128 devices in a mesh: dp: 8 (over z, core), seq: 8 (over x, y_lo), mp: 2 (over y_hi).
Axes of the slice: x: 4, y: 4 (y_hi: 2, y_lo: 2; y = y_hi * 2 + y_lo), z: 4, core: 2. Of those that a mesh axis runs over, the one named last changes fastest.
Arguments:
- residual: bfloat16 [24576, 3072], P(('dp', 'seq'), 'mp'), parts along dimension 0, may hold values from -10 to 10
- queries: bfloat16 [24576, 3072], P(('dp', 'seq', 'mp')), parts along dimension 0, may hold values from -6 to 6
- keys: bfloat16 [24576, 3072], P(('dp', 'seq', 'mp')), parts along dimension 0, may hold values from -6 to 6
- values: bfloat16 [24576, 3072], P(('dp', 'seq', 'mp')), parts along dimension 0, may hold values from -6 to 6
- video_ids: int32 [24576], P(('dp', 'seq', 'mp')), parts along dimension 0, may hold values from 0 to 3, never falling along the last dimension, each value on 1 to 1536 neighbouring positions
- timestep: int32 [8], P('dp'), parts along dimension 0, may hold values from 0 to 49
- modulation: float32 [50, 3, 3072], P(None, None, 'mp'), may hold values from -4 to 4
- out_weight: bfloat16 [3072, 3072], P(None, 'mp'), may hold values from -0.109375 to 0.109375
Outputs:
- hidden_out: bfloat16 [24576, 3072], P(('dp', 'seq'), 'mp'), parts along dimension 0
- mlp_input: bfloat16 [24576, 3072], P(('dp', 'seq'), 'mp'), parts along dimension 0
The draws below stay inside these ranges and needn't reach their ends.
There are 8 independent parts, one for each index of `dp`. The reference program is written for one: setup_inputs(seed, part) draws one part's arguments, and reference() takes and returns one part's arrays. A program takes and returns all parts, laid end to end along the dimension named above; an argument that names none is the same for every part. Nothing has to cross between parts.
Inputs may be any that keep to these rules, and one draw needn't show every extreme that they name: `video_ids`: video ids never fall along the tokens; each video holds 1 to 1536 tokens and one holds exactly 1536.
All inputs are finite; a program needn't handle non-finite values.
Results may differ from the reference program's by a relative error of at most 0.005.
Values may be sent and summed in bfloat16 or wider, within the bound.
No kernel may reach another device: no remote copies, remote signals or barrier semaphores. Data moves between devices by JAX's collectives and lax.ppermute only.
A program may use at most 256 MiB of HBM per device.

```python
import math
import jax
import jax.numpy as jnp
import numpy as np
from jax import lax

D = 3072
HEADS = 24
HEAD_DIM = 128
NSTEP = 50
VIDEOS = 4
TOKENS = 3072


def base_field(key):
    return 1.5 * jax.random.truncated_normal(key, -4.0, 4.0, (TOKENS, D), jnp.float32)


def draw_queries(key, part):
    field = base_field(jax.random.fold_in(key, 1))
    return field.astype(jnp.bfloat16)


def draw_keys(key, part):
    field = base_field(jax.random.fold_in(key, 2))
    return field.astype(jnp.bfloat16)


def draw_residual(key, part):
    columns = jnp.arange(D, dtype=jnp.float32)
    col_scale = 3.0 ** (columns / D) * jax.random.uniform(jax.random.fold_in(key, 3), (D,), jnp.float32, 0.6, 1.6)
    row_scale = jnp.exp(jax.random.uniform(jax.random.fold_in(key, 4), (TOKENS, 1), jnp.float32, math.log(0.05), math.log(0.5)))
    field = jax.random.truncated_normal(jax.random.fold_in(key, 5), -4.0, 4.0, (TOKENS, D), jnp.float32)
    return (field * row_scale * col_scale[None, :]).astype(jnp.bfloat16)


def block_scale(rng, dims, pieces, smallest, largest):
    gain, own = 1.0, jax.random.fold_in(rng, 6)
    for axis_at, shards_of in pieces:
        heights = jnp.exp(jax.random.uniform(jax.random.fold_in(own, axis_at), (shards_of,), jnp.float32, smallest / len(pieces), largest / len(pieces)))
        gain = gain * jnp.repeat(heights, dims[axis_at] // shards_of).reshape([-1 if axis == axis_at else 1 for axis in range(len(dims))])
    return gain


def split_up(amount, total, limit, slope):
    weights = [(1 << 20) // math.isqrt(rank ** slope) + 1 for rank in range(2, amount + 1)]
    rest, given = total - limit - (amount - 1), [1] * (amount - 1)
    while rest > 0:
        candidates = [i for i in range(amount - 1) if given[i] < limit]
        whole, remaining = sum([weights[i] for i in candidates]), rest
        for i in candidates:
            extra = min(limit - given[i], max(1, remaining * weights[i] // whole), rest)
            given[i] = given[i] + extra
            rest = rest - extra
    return np.array([limit] + given)


def uneven(stream_key, number_of, total, reach, skew):
    if number_of == 2:
        one = jax.random.randint(stream_key, (), max(1, total - reach), min(reach, total - 1) + 1)
        return jnp.stack([one, total - one])
    sizes = jnp.asarray(split_up(number_of, total, reach, skew), jnp.int32)
    twos = (number_of - 1) // 2
    donor, sink = sizes[1:1 + 2 * twos:2], sizes[2:2 + 2 * twos:2]
    slack = jnp.minimum(donor - 1, reach - sink)
    moved = jax.random.randint(jax.random.fold_in(stream_key, 1), (twos,), 0, 1 << 20) % (slack + 1)
    sizes = sizes.at[1:1 + 2 * twos:2].set(donor - moved).at[2:2 + 2 * twos:2].set(sink + moved)
    return sizes[jax.random.permutation(jax.random.fold_in(stream_key, 2), number_of)]


def noise(key, extent, scale, limit, shards=(), kind=jnp.bfloat16):
    gain = block_scale(key, extent, shards, -0.22, 0.18) if shards else 1.0
    result = jax.random.normal(key, extent, jnp.float32) * scale * gain
    return jnp.minimum(jnp.maximum(result, -limit), limit).astype(kind)


def setup_inputs(seed: int = 0, part: int = 0) -> dict:
    seeds = jax.random.split(jax.random.key(seed), 9)
    part_keys = jax.random.split(jax.random.fold_in(seeds[8], part), 9)
    return {
        "residual": draw_residual(jax.random.fold_in(jax.random.fold_in(seeds[8], part), 71), part),
        "queries": draw_queries(jax.random.fold_in(jax.random.fold_in(seeds[8], part), 71), part),
        "keys": draw_keys(jax.random.fold_in(jax.random.fold_in(seeds[8], part), 71), part),
        "values": noise(part_keys[3], (TOKENS, D), 1.0, 6.0, ((0, 16),)),
        "video_ids": jnp.searchsorted(jnp.cumsum(uneven(part_keys[4], VIDEOS, TOKENS, TOKENS // 2, 2)), jnp.arange(TOKENS), side="right").astype(jnp.int32),
        "timestep": jax.random.randint(part_keys[5], (1,), 0, NSTEP).astype(jnp.int32),
        "modulation": noise(seeds[6], (NSTEP, 3, D), 1.0, 4.0, ((2, 2),), jnp.float32),
        "out_weight": noise(seeds[7], (D, D), D ** -0.5, 0.109375, ((1, 2),)),
    }


def reference(residual, queries, keys, values, video_ids, timestep, modulation, out_weight):
    mod_rows = modulation[timestep[0]]
    gate = mod_rows[0]
    shift = mod_rows[1]
    scale = mod_rows[2]
    factor = 1.0 / HEAD_DIM ** 0.5
    same = video_ids[:, None] == video_ids[None, :]
    q_heads = queries.reshape(TOKENS, HEADS, HEAD_DIM).transpose(1, 0, 2)
    k_heads = keys.reshape(TOKENS, HEADS, HEAD_DIM).transpose(1, 0, 2)
    v_heads = values.reshape(TOKENS, HEADS, HEAD_DIM).transpose(1, 0, 2)

    def one_head(items):
        q_one, k_one, v_one = items
        score = jnp.dot(q_one, k_one.T, preferred_element_type=jnp.float32) * factor
        score = jnp.where(same, score, -1e+30)
        top = lax.optimization_barrier(jnp.max(score, axis=1, keepdims=True))
        weight = jnp.where(same, jnp.exp(score - top), 0.0)
        total = lax.optimization_barrier(jnp.sum(weight, axis=1, keepdims=True))
        summed = jnp.dot(weight.astype(jnp.bfloat16), v_one, preferred_element_type=jnp.float32)
        return summed / total
    per_head = lax.map(one_head, (q_heads, k_heads, v_heads))
    attended = per_head.transpose(1, 0, 2).reshape(TOKENS, D).astype(jnp.bfloat16)
    projected = jnp.dot(attended, out_weight, preferred_element_type=jnp.float32)
    stream = residual.astype(jnp.float32) + gate[None, :] * projected
    row_sum = lax.optimization_barrier(jnp.sum(stream, axis=1, keepdims=True))
    row_sq = lax.optimization_barrier(jnp.sum(stream * stream, axis=1, keepdims=True))
    mean = row_sum / D
    var = row_sq / D - mean * mean
    normed = (stream - mean) * lax.rsqrt(var + 1e-06) * (1.0 + scale[None, :]) + shift[None, :]
    return (stream.astype(jnp.bfloat16), normed.astype(jnp.bfloat16))
```

```python
import functools
import math

import jax
import jax.numpy as jnp
from jax import lax
from jax.experimental import pallas as pl
from jax.experimental.pallas import tpu as pltpu
from jax.sharding import PartitionSpec as P

HEAD_DIM = 128
SHARDS = 16
ROWS = 192
HALF = ROWS // 2
TOKENS = SHARDS * ROWS
QF, KF, KM, VF, VM, QM, ID = 0, 192, 384, 576, 768, 960, 1056
SENT = 1072
BACK = 3 * ROWS
TILE = 512
BIG = 32768.0
SCALE = math.log2(math.e) / math.sqrt(HEAD_DIM)
F32 = jnp.float32
BF16 = jnp.bfloat16


def pack_kernel(q_ref, k_ref, v_ref, id_ref, out_ref):
    for m in range(2):
        full = slice(2 * m * HEAD_DIM, (2 * m + 1) * HEAD_DIM)
        mid = slice(HEAD_DIM, 2 * HEAD_DIM)
        out_ref[m, QF:KF] = q_ref[:, full]
        out_ref[m, KF:KM] = k_ref[:, full]
        out_ref[m, KM:VF] = k_ref[:, mid]
        out_ref[m, VF:VM] = v_ref[:, full]
        out_ref[m, VM:QM] = v_ref[:, mid]
        out_ref[m, QM:ID] = q_ref[m * HALF : (m + 1) * HALF, mid]
        out_ref[m, ID:SENT] = id_ref[...]


def pack(queries, keys, values, id_rows):
    heads3 = pl.BlockSpec((ROWS, 3 * HEAD_DIM), lambda s: (0, s))
    return pl.pallas_call(
        pack_kernel,
        grid=(SHARDS // 2,),
        in_specs=[heads3, heads3, heads3, pl.BlockSpec((SENT - ID, HEAD_DIM), lambda s: (0, 0))],
        out_specs=pl.BlockSpec((2, SENT, HEAD_DIM), lambda s: (s, 0, 0)),
        out_shape=jax.ShapeDtypeStruct((SHARDS, SENT, HEAD_DIM), BF16),
        name="pack",
    )(queries, keys, values, id_rows)


def attend_kernel(mp_ref, got, out_ref, kf, km, vf, vm, qf, qm, ids, bounds, sem):
    t = pl.program_id(0)
    left = pl.ds(0, HEAD_DIM)
    right = pl.ds(HEAD_DIM, HEAD_DIM)

    @pl.when(t == 0)
    def _():
        copies = []
        for b in range(SHARDS):
            rows = pl.ds(b * ROWS, ROWS)
            half = pl.ds(b * HALF, HALF)
            for n, (first, count, ref, dst) in enumerate(
                (
                    (ID, SENT - ID, ids, None),
                    (QF, ROWS, qf, rows),
                    (QM, HALF, qm, half),
                    (KF, ROWS, kf, rows),
                    (KM, ROWS, km, rows),
                    (VF, ROWS, vf, rows),
                    (VM, ROWS, vm, rows),
                )
            ):
                to = ref.at[b] if dst is None else ref.at[dst, left]
                copy = pltpu.make_async_copy(got.at[b, pl.ds(first, count)], to, sem.at[n, b])
                copy.start()
                copies.append((n, copy))
        tail = pl.ds(TOKENS, TILE)
        for ref in (kf, km, vf, vm):
            ref[tail, left] = jnp.zeros((TILE, HEAD_DIM), BF16)
        for ref in (vf, vm):
            ref[:, right] = jnp.ones((TOKENS + TILE, HEAD_DIM), BF16)
        for n, copy in copies:
            if n == 0:
                copy.wait()
        every = ids[...].astype(F32)
        for v in range(3):
            bounds[v] = jnp.sum((every <= v + 0.5).astype(F32)).astype(jnp.int32)
        lane = lax.broadcasted_iota(jnp.int32, (1, HEAD_DIM), 1)
        c0, c1, c2 = bounds[0], bounds[1], bounds[2]
        low = jnp.where(lane == 0, 0, jnp.where(lane == 1, c0, jnp.where(lane == 2, c1, c2)))
        high = jnp.where(lane == 0, c0, jnp.where(lane == 1, c1, jnp.where(lane == 2, c2, TOKENS)))
        none = lane > 3

        def fill(i, _):
            rows = pl.ds(pl.multiple_of(i * ROWS, ROWS), ROWS)
            token = lax.broadcasted_iota(jnp.int32, (ROWS, HEAD_DIM), 0) + i * ROWS
            inside = (token >= low) & (token < high)
            key = jnp.where(inside | none, 0.0, -BIG).astype(BF16)
            kf[rows, right] = key
            km[rows, right] = key
            qf[rows, right] = jnp.where(inside & ~none, 1.0, 0.0).astype(BF16)
            half = pl.ds(pl.multiple_of(i * HALF, HALF), HALF)
            mine = pl.ds(pl.multiple_of(i * ROWS + mp_ref[0] * HALF, HALF), HALF)
            qm[half, right] = qf[mine, right]
            return 0

        lax.fori_loop(0, SHARDS, fill, 0)
        outside = jnp.where(lane > 3, 0.0, -BIG).astype(BF16)
        for ref in (kf, km):
            ref[tail, right] = jnp.broadcast_to(outside, (TILE, HEAD_DIM))
        for n, copy in copies:
            if n:
                copy.wait()

    c0, c1, c2 = bounds[0], bounds[1], bounds[2]
    first = t * (2 * ROWS)
    last = first + (2 * ROWS - 1)
    low = jnp.where(first >= c2, c2, jnp.where(first >= c1, c1, jnp.where(first >= c0, c0, 0)))
    high = jnp.where(last < c0, c0, jnp.where(last < c1, c1, jnp.where(last < c2, c2, TOKENS)))
    low = (low // 16) * 16
    steps = (high - low + TILE - 1) // TILE

    q_full = qf[pl.ds(pl.multiple_of(first, 2 * ROWS), 2 * ROWS), :]
    q_mid = qm[pl.ds(pl.multiple_of(t * ROWS, ROWS), ROWS), :]

    def one(q, k, v, top, acc):
        score = lax.dot_general(q, k, (((1,), (1,)), ((), ())), preferred_element_type=F32)
        peak = jnp.maximum(top, jnp.max(score, axis=1, keepdims=True))
        weight = jnp.exp2((score - peak) * SCALE).astype(BF16)
        kept = jnp.exp2((top - peak) * SCALE)
        return peak, acc * kept + jnp.dot(weight, v, preferred_element_type=F32)

    def step(i, carry):
        top_full, acc_full, top_mid, acc_mid = carry
        at = pl.ds(pl.multiple_of(low + i * TILE, 16), TILE)
        return one(q_full, kf[at, :], vf[at, :], top_full, acc_full) + one(q_mid, km[at, :], vm[at, :], top_mid, acc_mid)

    start = []
    for rows in (2 * ROWS, ROWS):
        start += [jnp.full((rows, 1), -1e30, F32), jnp.zeros((rows, 2 * HEAD_DIM), F32)]
    _, acc_full, _, acc_mid = lax.fori_loop(0, steps, step, tuple(start))
    for acc, at in ((acc_full, slice(0, 2 * ROWS)), (acc_mid, slice(2 * ROWS, BACK))):
        result = (acc[:, :HEAD_DIM] / acc[:, HEAD_DIM:]).astype(BF16)
        out_ref[0, at] = result
        out_ref[1, at] = result


def attend(mp_index, got):
    long = pltpu.VMEM((TOKENS + TILE, 2 * HEAD_DIM), BF16)
    return pl.pallas_call(
        attend_kernel,
        grid=(SHARDS // 2,),
        in_specs=[pl.BlockSpec(memory_space=pltpu.SMEM), pl.BlockSpec(memory_space=pl.ANY)],
        out_specs=pl.BlockSpec((2, BACK, HEAD_DIM), lambda t: (t, 0, 0)),
        out_shape=jax.ShapeDtypeStruct((SHARDS, BACK, HEAD_DIM), BF16),
        scratch_shapes=[
            long,
            long,
            long,
            long,
            pltpu.VMEM((TOKENS, 2 * HEAD_DIM), BF16),
            pltpu.VMEM((TOKENS // 2, 2 * HEAD_DIM), BF16),
            pltpu.VMEM((SHARDS, SENT - ID, HEAD_DIM), BF16),
            pltpu.SMEM((4,), jnp.int32),
            pltpu.SemaphoreType.DMA((7, SHARDS)),
        ],
        name="attend",
    )(mp_index, got)


def project_kernel(got, w_ref, res_ref, mod_ref, hidden_ref, stream_ref, stat_ref, attended, sums):
    j = pl.program_id(0)

    @pl.when(j == 0)
    def _():
        for s in range(SHARDS // 2):
            mid = slice((3 * s + 1) * HEAD_DIM, (3 * s + 2) * HEAD_DIM)
            for m in range(2):
                full = slice((3 * s + 2 * m) * HEAD_DIM, (3 * s + 2 * m + 1) * HEAD_DIM)
                d = 2 * s + m
                attended[:, full] = got[d, : 2 * ROWS]
                for b in range(2):
                    attended[b * ROWS + m * HALF : b * ROWS + (m + 1) * HALF, mid] = got[
                        d, 2 * ROWS + b * HALF : 2 * ROWS + (b + 1) * HALF
                    ]
        sums[...] = jnp.zeros_like(sums)

    projected = jnp.dot(attended[...], w_ref[...], preferred_element_type=F32)
    stream = res_ref[...].astype(F32) + mod_ref[0:1, :] * projected
    hidden_ref[...] = stream.astype(BF16)
    stream_ref[...] = stream
    one, two = sums[0], sums[1]
    for c in range(stream.shape[1] // HEAD_DIM):
        part = stream[:, c * HEAD_DIM : (c + 1) * HEAD_DIM]
        one = one + part
        two = two + part * part
    sums[0] = one
    sums[1] = two

    @pl.when(j == pl.num_programs(0) - 1)
    def _():
        stat_ref[...] = jnp.zeros_like(stat_ref)
        stat_ref[0:1, :] = jnp.sum(sums[0].T, axis=0, keepdims=True)
        stat_ref[1:2, :] = jnp.sum(sums[1].T, axis=0, keepdims=True)


def project(got, out_weight, residual, mod_rows):
    width, cols = out_weight.shape
    rows = residual.shape[0]
    block = 512
    column = lambda j: (0, j)
    return pl.pallas_call(
        project_kernel,
        grid=(cols // block,),
        in_specs=[
            pl.BlockSpec((SHARDS, BACK, HEAD_DIM), lambda j: (0, 0, 0)),
            pl.BlockSpec((width, block), column),
            pl.BlockSpec((rows, block), column),
            pl.BlockSpec((3, block), column),
        ],
        out_specs=[
            pl.BlockSpec((rows, block), column),
            pl.BlockSpec((rows, block), column),
            pl.BlockSpec((8, rows), lambda j: (0, 0)),
        ],
        out_shape=[
            jax.ShapeDtypeStruct((rows, cols), BF16),
            jax.ShapeDtypeStruct((rows, cols), F32),
            jax.ShapeDtypeStruct((8, rows), F32),
        ],
        scratch_shapes=[pltpu.VMEM((rows, width), BF16), pltpu.VMEM((2, rows, HEAD_DIM), F32)],
        name="project",
    )(got, out_weight, residual, mod_rows)


def norm_kernel(width, stream_ref, mine_ref, other_ref, mod_ref, out_ref):
    stats = mine_ref[...] + other_ref[...]
    mean = stats[0:1, :] / width
    var = stats[1:2, :] / width - mean * mean
    rows = mean.shape[1]
    mean = jnp.broadcast_to(mean, (HEAD_DIM, rows)).T
    inv = jnp.broadcast_to(lax.rsqrt(var + 1e-06), (HEAD_DIM, rows)).T
    for c in range(stream_ref.shape[1] // HEAD_DIM):
        at = slice(c * HEAD_DIM, (c + 1) * HEAD_DIM)
        shift = mod_ref[1:2, at]
        scale = mod_ref[2:3, at]
        out_ref[:, at] = ((stream_ref[:, at] - mean) * inv * (1.0 + scale) + shift).astype(BF16)


def norm(stream, mine, other, mod_rows, width):
    rows, cols = stream.shape
    block = 768
    column = lambda j: (0, j)
    whole = pl.BlockSpec((8, rows), lambda j: (0, 0))
    return pl.pallas_call(
        functools.partial(norm_kernel, width),
        grid=(cols // block,),
        in_specs=[pl.BlockSpec((rows, block), column), whole, whole, pl.BlockSpec((3, block), column)],
        out_specs=pl.BlockSpec((rows, block), column),
        out_shape=jax.ShapeDtypeStruct((rows, cols), BF16),
        name="norm",
    )(stream, mine, other, mod_rows)


def local(residual, queries, keys, values, video_ids, timestep, modulation, out_weight):
    axes = ("seq", "mp")
    mod_rows = lax.dynamic_index_in_dim(modulation, timestep[0], 0, keepdims=False)
    spare = jnp.full(((SENT - ID) * HEAD_DIM - ROWS,), 7, jnp.int32)
    id_rows = jnp.concatenate([video_ids, spare]).reshape(SENT - ID, HEAD_DIM).astype(BF16)
    got = lax.all_to_all(pack(queries, keys, values, id_rows), axes, 0, 0)
    mp_index = lax.axis_index("mp").astype(jnp.int32).reshape(1)
    back = lax.all_to_all(attend(mp_index, got), axes, 0, 0)
    hidden, stream, mine = project(back, out_weight, residual, mod_rows)
    other = lax.ppermute(mine, "mp", [(0, 1), (1, 0)])
    return hidden, norm(stream, mine, other, mod_rows, queries.shape[1])


def solution(mesh):
    return jax.shard_map(
        local,
        mesh=mesh,
        in_specs=(
            P(("dp", "seq"), "mp"),
            P(("dp", "seq", "mp"), None),
            P(("dp", "seq", "mp"), None),
            P(("dp", "seq", "mp"), None),
            P(("dp", "seq", "mp")),
            P("dp"),
            P(None, None, "mp"),
            P(None, "mp"),
        ),
        out_specs=(P(("dp", "seq"), "mp"), P(("dp", "seq"), "mp")),
        check_vma=False,
    )
```

```python
import functools
import math

import jax
import jax.numpy as jnp
from jax import lax
from jax.experimental import pallas as pl
from jax.experimental.pallas import tpu as pltpu
from jax.sharding import PartitionSpec as P

HEAD_DIM = 128
SHARDS = 16
ROWS = 192
HALF = ROWS // 2
TOKENS = SHARDS * ROWS
QF, KF, KM, VF, VM, QM, ID = 0, 192, 384, 576, 768, 960, 1056
SENT = 1072
BACK = 3 * ROWS
TILE = 512
BIG = 32768.0
SCALE = math.log2(math.e) / math.sqrt(HEAD_DIM)
F32 = jnp.float32
BF16 = jnp.bfloat16


def pack_kernel(q_ref, k_ref, v_ref, id_ref, out_ref):
    for m in range(2):
        full = slice(2 * m * HEAD_DIM, (2 * m + 1) * HEAD_DIM)
        mid = slice(HEAD_DIM, 2 * HEAD_DIM)
        out_ref[m, QF:KF] = q_ref[:, full]
        out_ref[m, KF:KM] = k_ref[:, full]
        out_ref[m, KM:VF] = k_ref[:, mid]
        out_ref[m, VF:VM] = v_ref[:, full]
        out_ref[m, VM:QM] = v_ref[:, mid]
        out_ref[m, QM:ID] = q_ref[m * HALF : (m + 1) * HALF, mid]
        out_ref[m, ID:SENT] = id_ref[...]


def pack(queries, keys, values, id_rows):
    heads3 = pl.BlockSpec((ROWS, 3 * HEAD_DIM), lambda s: (0, s))
    return pl.pallas_call(
        pack_kernel,
        grid=(SHARDS // 2,),
        in_specs=[heads3, heads3, heads3, pl.BlockSpec((SENT - ID, HEAD_DIM), lambda s: (0, 0))],
        out_specs=pl.BlockSpec((2, SENT, HEAD_DIM), lambda s: (s, 0, 0)),
        out_shape=jax.ShapeDtypeStruct((SHARDS, SENT, HEAD_DIM), BF16),
        name="pack",
    )(queries, keys, values, id_rows)


def attend_kernel(mp_ref, got, out_ref, kf, km, vf, vm, qf, qm, ids, bounds, sem):
    t = pl.program_id(0)
    left = pl.ds(0, HEAD_DIM)
    right = pl.ds(HEAD_DIM, HEAD_DIM)

    @pl.when(t == 0)
    def _():
        copies = []
        for b in range(SHARDS):
            rows = pl.ds(b * ROWS, ROWS)
            half = pl.ds(b * HALF, HALF)
            for n, (first, count, ref, dst) in enumerate(
                (
                    (ID, SENT - ID, ids, None),
                    (QF, ROWS, qf, rows),
                    (QM, HALF, qm, half),
                    (KF, ROWS, kf, rows),
                    (KM, ROWS, km, rows),
                    (VF, ROWS, vf, rows),
                    (VM, ROWS, vm, rows),
                )
            ):
                to = ref.at[b] if dst is None else ref.at[dst, left]
                copy = pltpu.make_async_copy(got.at[b, pl.ds(first, count)], to, sem.at[n, b])
                copy.start()
                copies.append((n, copy))
        tail = pl.ds(TOKENS, TILE)
        for ref in (kf, km, vf, vm):
            ref[tail, left] = jnp.zeros((TILE, HEAD_DIM), BF16)
        for ref in (vf, vm):
            ref[:, right] = jnp.ones((TOKENS + TILE, HEAD_DIM), BF16)
        for n, copy in copies:
            if n == 0:
                copy.wait()
        every = ids[...].astype(F32)
        for v in range(3):
            bounds[v] = jnp.sum((every <= v + 0.5).astype(F32)).astype(jnp.int32)
        lane = lax.broadcasted_iota(jnp.int32, (1, HEAD_DIM), 1)
        c0, c1, c2 = bounds[0], bounds[1], bounds[2]
        low = jnp.where(lane == 0, 0, jnp.where(lane == 1, c0, jnp.where(lane == 2, c1, c2)))
        high = jnp.where(lane == 0, c0, jnp.where(lane == 1, c1, jnp.where(lane == 2, c2, TOKENS)))
        none = lane > 3

        def fill(i, _):
            rows = pl.ds(pl.multiple_of(i * ROWS, ROWS), ROWS)
            token = lax.broadcasted_iota(jnp.int32, (ROWS, HEAD_DIM), 0) + i * ROWS
            inside = (token >= low) & (token < high)
            key = jnp.where(inside | none, 0.0, -BIG).astype(BF16)
            kf[rows, right] = key
            km[rows, right] = key
            qf[rows, right] = jnp.where(inside & ~none, 1.0, 0.0).astype(BF16)
            half = pl.ds(pl.multiple_of(i * HALF, HALF), HALF)
            mine = pl.ds(pl.multiple_of(i * ROWS + mp_ref[0] * HALF, HALF), HALF)
            qm[half, right] = qf[mine, right]
            return 0

        lax.fori_loop(0, SHARDS, fill, 0)
        outside = jnp.where(lane > 3, 0.0, -BIG).astype(BF16)
        for ref in (kf, km):
            ref[tail, right] = jnp.broadcast_to(outside, (TILE, HEAD_DIM))
        for n, copy in copies:
            if n:
                copy.wait()

    c0, c1, c2 = bounds[0], bounds[1], bounds[2]
    first = t * (2 * ROWS)
    last = first + (2 * ROWS - 1)
    low = jnp.where(first >= c2, c2, jnp.where(first >= c1, c1, jnp.where(first >= c0, c0, 0)))
    high = jnp.where(last < c0, c0, jnp.where(last < c1, c1, jnp.where(last < c2, c2, TOKENS)))
    low = (low // 16) * 16
    steps = (high - low + TILE - 1) // TILE

    q_full = qf[pl.ds(pl.multiple_of(first, 2 * ROWS), 2 * ROWS), :]
    q_mid = qm[pl.ds(pl.multiple_of(t * ROWS, ROWS), ROWS), :]

    def one(q, k, v, top, acc):
        score = lax.dot_general(q, k, (((1,), (1,)), ((), ())), preferred_element_type=F32)
        peak = jnp.maximum(top, jnp.max(score, axis=1, keepdims=True))
        weight = jnp.exp2((score - peak) * SCALE).astype(BF16)
        kept = jnp.exp2((top - peak) * SCALE)
        return peak, acc * kept + jnp.dot(weight, v, preferred_element_type=F32)

    def step(i, carry):
        top_full, acc_full, top_mid, acc_mid = carry
        at = pl.ds(pl.multiple_of(low + i * TILE, 16), TILE)
        return one(q_full, kf[at, :], vf[at, :], top_full, acc_full) + one(q_mid, km[at, :], vm[at, :], top_mid, acc_mid)

    start = []
    for rows in (2 * ROWS, ROWS):
        start += [jnp.full((rows, 1), -1e30, F32), jnp.zeros((rows, 2 * HEAD_DIM), F32)]
    _, acc_full, _, acc_mid = lax.fori_loop(0, steps, step, tuple(start))
    for acc, at in ((acc_full, slice(0, 2 * ROWS)), (acc_mid, slice(2 * ROWS, BACK))):
        result = (acc[:, :HEAD_DIM] / acc[:, HEAD_DIM:]).astype(BF16)
        out_ref[0, at] = result
        out_ref[1, at] = result


def attend(mp_index, got):
    long = pltpu.VMEM((TOKENS + TILE, 2 * HEAD_DIM), BF16)
    return pl.pallas_call(
        attend_kernel,
        grid=(SHARDS // 2,),
        in_specs=[pl.BlockSpec(memory_space=pltpu.SMEM), pl.BlockSpec(memory_space=pl.ANY)],
        out_specs=pl.BlockSpec((2, BACK, HEAD_DIM), lambda t: (t, 0, 0)),
        out_shape=jax.ShapeDtypeStruct((SHARDS, BACK, HEAD_DIM), BF16),
        scratch_shapes=[
            long,
            long,
            long,
            long,
            pltpu.VMEM((TOKENS, 2 * HEAD_DIM), BF16),
            pltpu.VMEM((TOKENS // 2, 2 * HEAD_DIM), BF16),
            pltpu.VMEM((SHARDS, SENT - ID, HEAD_DIM), BF16),
            pltpu.SMEM((4,), jnp.int32),
            pltpu.SemaphoreType.DMA((7, SHARDS)),
        ],
        name="attend",
    )(mp_index, got)


def project_kernel(got, w_ref, res_ref, mod_ref, hidden_ref, stream_ref, stat_ref, attended, sums):
    j = pl.program_id(0)

    @pl.when(j == 0)
    def _():
        for s in range(SHARDS // 2):
            mid = slice((3 * s + 1) * HEAD_DIM, (3 * s + 2) * HEAD_DIM)
            for m in range(2):
                full = slice((3 * s + 2 * m) * HEAD_DIM, (3 * s + 2 * m + 1) * HEAD_DIM)
                d = 2 * s + m
                attended[:, full] = got[d, : 2 * ROWS]
                for b in range(2):
                    attended[b * ROWS + m * HALF : b * ROWS + (m + 1) * HALF, mid] = got[
                        d, 2 * ROWS + b * HALF : 2 * ROWS + (b + 1) * HALF
                    ]
        sums[...] = jnp.zeros_like(sums)

    projected = jnp.dot(attended[...], w_ref[...], preferred_element_type=F32)
    stream = res_ref[...].astype(F32) + mod_ref[0:1, :] * projected
    hidden_ref[...] = stream.astype(BF16)
    stream_ref[...] = stream
    one, two = sums[0], sums[1]
    for c in range(stream.shape[1] // HEAD_DIM):
        part = stream[:, c * HEAD_DIM : (c + 1) * HEAD_DIM]
        one = one + part
        two = two + part * part
    sums[0] = one
    sums[1] = two

    @pl.when(j == pl.num_programs(0) - 1)
    def _():
        stat_ref[...] = jnp.zeros_like(stat_ref)
        stat_ref[0:1, :] = jnp.sum(sums[0].T, axis=0, keepdims=True)
        stat_ref[1:2, :] = jnp.sum(sums[1].T, axis=0, keepdims=True)


def project(got, out_weight, residual, mod_rows):
    width, cols = out_weight.shape
    rows = residual.shape[0]
    block = 512
    column = lambda j: (0, j)
    return pl.pallas_call(
        project_kernel,
        grid=(cols // block,),
        in_specs=[
            pl.BlockSpec((SHARDS, BACK, HEAD_DIM), lambda j: (0, 0, 0)),
            pl.BlockSpec((width, block), column),
            pl.BlockSpec((rows, block), column),
            pl.BlockSpec((3, block), column),
        ],
        out_specs=[
            pl.BlockSpec((rows, block), column),
            pl.BlockSpec((rows, block), column),
            pl.BlockSpec((8, rows), lambda j: (0, 0)),
        ],
        out_shape=[
            jax.ShapeDtypeStruct((rows, cols), BF16),
            jax.ShapeDtypeStruct((rows, cols), F32),
            jax.ShapeDtypeStruct((8, rows), F32),
        ],
        scratch_shapes=[pltpu.VMEM((rows, width), BF16), pltpu.VMEM((2, rows, HEAD_DIM), F32)],
        name="project",
    )(got, out_weight, residual, mod_rows)


def norm_kernel(width, stream_ref, mine_ref, other_ref, mod_ref, out_ref):
    stats = mine_ref[...] + other_ref[...]
    mean = stats[0:1, :] / width
    var = stats[1:2, :] / width - mean * mean
    rows = mean.shape[1]
    mean = jnp.broadcast_to(mean, (HEAD_DIM, rows)).T
    inv = jnp.broadcast_to(lax.rsqrt(var + 1e-06), (HEAD_DIM, rows)).T
    for c in range(stream_ref.shape[1] // HEAD_DIM):
        at = slice(c * HEAD_DIM, (c + 1) * HEAD_DIM)
        shift = mod_ref[1:2, at]
        scale = mod_ref[2:3, at]
        out_ref[:, at] = ((stream_ref[:, at] - mean) * inv * (1.0 + scale) + shift).astype(BF16)


def norm(stream, mine, other, mod_rows, width):
    rows, cols = stream.shape
    block = 768
    column = lambda j: (0, j)
    whole = pl.BlockSpec((8, rows), lambda j: (0, 0))
    return pl.pallas_call(
        functools.partial(norm_kernel, width),
        grid=(cols // block,),
        in_specs=[pl.BlockSpec((rows, block), column), whole, whole, pl.BlockSpec((3, block), column)],
        out_specs=pl.BlockSpec((rows, block), column),
        out_shape=jax.ShapeDtypeStruct((rows, cols), BF16),
        name="norm",
    )(stream, mine, other, mod_rows)


def local(residual, queries, keys, values, video_ids, timestep, modulation, out_weight):
    axes = ("seq", "mp")
    mod_rows = lax.dynamic_index_in_dim(modulation, timestep[0], 0, keepdims=False)
    spare = jnp.full(((SENT - ID) * HEAD_DIM - ROWS,), 7, jnp.int32)
    id_rows = jnp.concatenate([video_ids, spare]).reshape(SENT - ID, HEAD_DIM).astype(BF16)
    mp_index = lax.axis_index("mp").astype(jnp.int32).reshape(1)
    packed, mp_index, mod_rows = lax.optimization_barrier(
        (pack(queries, keys, values, id_rows), mp_index, mod_rows)
    )
    got = lax.all_to_all(packed, axes, 0, 0)
    back = lax.all_to_all(attend(mp_index, got), axes, 0, 0)
    hidden, stream, mine = project(back, out_weight, residual, mod_rows)
    other = lax.ppermute(mine, "mp", [(0, 1), (1, 0)])
    return hidden, norm(stream, mine, other, mod_rows, queries.shape[1])


def solution(mesh):
    return jax.shard_map(
        local,
        mesh=mesh,
        in_specs=(
            P(("dp", "seq"), "mp"),
            P(("dp", "seq", "mp"), None),
            P(("dp", "seq", "mp"), None),
            P(("dp", "seq", "mp"), None),
            P(("dp", "seq", "mp")),
            P("dp"),
            P(None, None, "mp"),
            P(None, "mp"),
        ),
        out_specs=(P(("dp", "seq"), "mp"), P(("dp", "seq"), "mp")),
        check_vma=False,
    )
```

```python
import functools
import math

import jax
import jax.numpy as jnp
from jax import lax
from jax.experimental import pallas as pl
from jax.experimental.pallas import tpu as pltpu
from jax.sharding import PartitionSpec as P

HEAD_DIM = 128
SHARDS = 16
ROWS = 192
HALF = ROWS // 2
TOKENS = SHARDS * ROWS
QF, KF, KM, VF, VM, QM, ID = 0, 192, 384, 576, 768, 960, 1056
SENT = 1072
BACK = 3 * ROWS
TILE = 512
SPARE = -(-TILE // ROWS)
BIG = 32768.0
SCALE = math.log2(math.e) / math.sqrt(HEAD_DIM)
F32 = jnp.float32
BF16 = jnp.bfloat16


def pieces(s, m):
    full, mid = 3 * s + 2 * m, 3 * s + 1
    return (
        (0, QF, ROWS, 0, full),
        (1, KF, ROWS, 0, full),
        (1, KM, ROWS, 0, mid),
        (2, VF, ROWS, 0, full),
        (2, VM, ROWS, 0, mid),
        (0, QM, HALF, m * HALF, mid),
    )


def pack_kernel(q_ref, k_ref, v_ref, id_ref, out_ref, sem):
    given = (q_ref, k_ref, v_ref)
    for s in range(SHARDS // 2):
        for m in range(2):
            for which, to, count, row, head in pieces(s, m):
                source = given[which].at[pl.ds(row, count), pl.ds(head * HEAD_DIM, HEAD_DIM)]
                pltpu.make_async_copy(source, out_ref.at[2 * s + m, pl.ds(to, count)], sem).start()
            pltpu.make_async_copy(id_ref, out_ref.at[2 * s + m, pl.ds(ID, SENT - ID)], sem).start()
    pltpu.make_async_copy(out_ref, out_ref, sem).wait()


def pack(queries, keys, values, id_rows):
    anywhere = pl.BlockSpec(memory_space=pl.ANY)
    return pl.pallas_call(
        pack_kernel,
        in_specs=[anywhere] * 4,
        out_specs=pl.BlockSpec(memory_space=pltpu.VMEM),
        out_shape=pltpu.VMEM((SHARDS, SENT, HEAD_DIM), BF16),
        scratch_shapes=[pltpu.SemaphoreType.DMA],
        compiler_params=pltpu.CompilerParams(vmem_limit_bytes=1 << 20),
        name="pack",
    )(queries, keys, values, id_rows)


def attend_kernel(mp_ref, got, out_ref, qf, qm, kf, km, vf, vm, ids, is_q, is_m, is_k, score, peak, top, acc, bounds, sem):
    copies = []
    for n, (first, count, ref) in enumerate(
        (
            (ID, SENT - ID, ids),
            (QF, ROWS, qf),
            (QM, HALF, qm),
            (KF, ROWS, kf),
            (KM, ROWS, km),
            (VF, ROWS, vf),
            (VM, ROWS, vm),
        )
    ):
        copy = pltpu.make_async_copy(got.at[:, pl.ds(first, count)], ref.at[pl.ds(0, SHARDS)], sem.at[n])
        copy.start()
        copies.append(copy)
    for ref in (kf, km, vf, vm):
        ref[SHARDS:] = jnp.zeros((SPARE, ROWS, HEAD_DIM), BF16)
    acc[...] = jnp.zeros_like(acc)
    top[...] = jnp.zeros_like(top)
    copies[0].wait()
    every = ids[...].astype(F32)
    for v in range(3):
        bounds[v] = jnp.sum((every <= v + 0.5).astype(F32)).astype(jnp.int32)
    c0, c1, c2 = bounds[0], bounds[1], bounds[2]
    lane = lax.broadcasted_iota(jnp.int32, (1, HEAD_DIM), 1)
    low_of = jnp.where(lane == 1, c0, jnp.where(lane == 2, c1, jnp.where(lane == 3, c2, 0)))
    end = TOKENS + SPARE * ROWS
    high_of = jnp.where(lane == 0, c0, jnp.where(lane == 1, c1, jnp.where(lane == 2, c2, jnp.where(lane == 3, TOKENS, end))))

    def inside(first, count):
        token = lax.broadcasted_iota(jnp.int32, (count, HEAD_DIM), 0) + first
        return (token >= low_of) & (token < high_of)

    def fill(b, _):
        here = inside(b * ROWS, ROWS)
        is_k[b] = jnp.where(here, 0.0, -BIG).astype(BF16)
        is_q[b] = jnp.where(here, 1.0, 0.0).astype(BF16)
        is_m[b] = jnp.where(inside(b * ROWS + mp_ref[0] * HALF, HALF), 1.0, 0.0).astype(BF16)
        return 0

    lax.fori_loop(0, SHARDS, fill, 0)
    for b in range(SHARDS, SHARDS + SPARE):
        is_k[b] = jnp.where(inside(b * ROWS, ROWS), 0.0, -BIG).astype(BF16)
    for copy in copies[1:]:
        copy.wait()

    def span(t):
        first = t * (2 * ROWS)
        last = first + (2 * ROWS - 1)
        low = jnp.where(first >= c2, c2, jnp.where(first >= c1, c1, jnp.where(first >= c0, c0, 0)))
        high = jnp.where(last < c0, c0, jnp.where(last < c1, c1, jnp.where(last < c2, c2, TOKENS)))
        low = (low // 16) * 16
        return low, (high - low + TILE - 1) // TILE

    def flat(ref):
        return ref.reshape(ref.shape[0] * ref.shape[1], HEAD_DIM)

    parts = ((slice(0, 2 * ROWS), qf, is_q, kf, vf), (slice(2 * ROWS, BACK), qm, is_m, km, vm))

    def look(t, key, slot):
        at = pl.ds(pl.multiple_of(key, 16), TILE)
        same = flat(is_k)[at, :]
        for rows, q_ref, is_ref, k_ref, _ in parts:
            count = rows.stop - rows.start
            mine = pl.ds(pl.multiple_of(t * count, count), count)
            q = jnp.concatenate([flat(q_ref)[mine, :], flat(is_ref)[mine, :]], axis=1)
            k = jnp.concatenate([flat(k_ref)[at, :], same], axis=1)
            found = lax.dot_general(q, k, (((1,), (1,)), ((), ())), preferred_element_type=F32)
            score[slot, rows] = found
            peak[slot, rows] = jnp.broadcast_to(jnp.max(found, axis=1, keepdims=True), (count, HEAD_DIM))

    def step(carry, slot):
        t, i = carry
        low, steps = span(t)
        done = i + 1 == steps
        next_t = jnp.where(done, t + 1, t)
        next_i = jnp.where(done, 0, i + 1)
        look_t = jnp.minimum(next_t, SHARDS // 2 - 1)
        look(look_t, span(look_t)[0] + next_i * TILE, 1 - slot)
        at = pl.ds(pl.multiple_of(low + i * TILE, 16), TILE)
        ones = jnp.ones((TILE, HEAD_DIM), BF16)
        for rows, _, _, _, v_ref in parts:
            old = jnp.where(i == 0, -1e30, top[rows])
            new = jnp.maximum(old, peak[slot, rows])
            top[rows] = new
            kept = jnp.exp2((old - new) * SCALE)
            weight = jnp.concatenate(
                [
                    jnp.exp2((score[slot, rows, c : c + HEAD_DIM] - new) * SCALE).astype(BF16)
                    for c in range(0, TILE, HEAD_DIM)
                ],
                axis=1,
            )
            v = jnp.concatenate([flat(v_ref)[at, :], ones], axis=1)
            more = jnp.dot(weight, v, preferred_element_type=F32)
            acc[rows] = acc[rows] * jnp.concatenate([kept, kept], axis=1) + more

        @pl.when(done & (t < SHARDS // 2))
        def _():
            result = (acc[:, :HEAD_DIM] / acc[:, HEAD_DIM:]).astype(BF16)
            out_ref[2 * t] = result
            out_ref[2 * t + 1] = result

        return next_t, next_i

    total = sum(span(t)[1] for t in range(SHARDS // 2))
    look(0, 0, 0)
    lax.fori_loop(0, (total + 1) // 2, lambda _, carry: step(step(carry, 0), 1), (0, 0))


def attend(mp_index, got):
    rows = lambda n, spare: pltpu.VMEM((SHARDS + spare, n, HEAD_DIM), BF16)
    return pl.pallas_call(
        attend_kernel,
        in_specs=[pl.BlockSpec(memory_space=pltpu.SMEM), pl.BlockSpec(memory_space=pl.ANY)],
        out_shape=jax.ShapeDtypeStruct((SHARDS, BACK, HEAD_DIM), BF16),
        scratch_shapes=[
            rows(ROWS, 0),
            rows(HALF, 0),
            rows(ROWS, SPARE),
            rows(ROWS, SPARE),
            rows(ROWS, SPARE),
            rows(ROWS, SPARE),
            rows(SENT - ID, 0),
            rows(ROWS, 0),
            rows(HALF, 0),
            rows(ROWS, SPARE),
            pltpu.VMEM((2, BACK, TILE), F32),
            pltpu.VMEM((2, BACK, HEAD_DIM), F32),
            pltpu.VMEM((BACK, HEAD_DIM), F32),
            pltpu.VMEM((BACK, 2 * HEAD_DIM), F32),
            pltpu.SMEM((4,), jnp.int32),
            pltpu.SemaphoreType.DMA((7,)),
        ],
        compiler_params=pltpu.CompilerParams(vmem_limit_bytes=20 << 20),
        name="attend",
    )(mp_index, got)


def project_kernel(got, w_ref, res_ref, mod_ref, hidden_ref, stream_ref, stat_ref, attended, sums):
    j = pl.program_id(0)

    @pl.when(j == 0)
    def _():
        for s in range(SHARDS // 2):
            mid = slice((3 * s + 1) * HEAD_DIM, (3 * s + 2) * HEAD_DIM)
            for m in range(2):
                full = slice((3 * s + 2 * m) * HEAD_DIM, (3 * s + 2 * m + 1) * HEAD_DIM)
                d = 2 * s + m
                attended[:, full] = got[d, : 2 * ROWS]
                for b in range(2):
                    attended[b * ROWS + m * HALF : b * ROWS + (m + 1) * HALF, mid] = got[
                        d, 2 * ROWS + b * HALF : 2 * ROWS + (b + 1) * HALF
                    ]
        sums[...] = jnp.zeros_like(sums)

    projected = jnp.dot(attended[...], w_ref[...], preferred_element_type=F32)
    stream = res_ref[...].astype(F32) + mod_ref[0:1, :] * projected
    hidden_ref[...] = stream.astype(BF16)
    stream_ref[...] = stream
    one, two = sums[0], sums[1]
    for c in range(stream.shape[1] // HEAD_DIM):
        part = stream[:, c * HEAD_DIM : (c + 1) * HEAD_DIM]
        one = one + part
        two = two + part * part
    sums[0] = one
    sums[1] = two

    @pl.when(j == pl.num_programs(0) - 1)
    def _():
        stat_ref[...] = jnp.zeros_like(stat_ref)
        stat_ref[0:1, :] = jnp.sum(sums[0].T, axis=0, keepdims=True)
        stat_ref[1:2, :] = jnp.sum(sums[1].T, axis=0, keepdims=True)


def project(got, out_weight, residual, mod_rows):
    width, cols = out_weight.shape
    rows = residual.shape[0]
    block = 512
    column = lambda j: (0, j)
    return pl.pallas_call(
        project_kernel,
        grid=(cols // block,),
        in_specs=[
            pl.BlockSpec((SHARDS, BACK, HEAD_DIM), lambda j: (0, 0, 0)),
            pl.BlockSpec((width, block), column),
            pl.BlockSpec((rows, block), column),
            pl.BlockSpec((3, block), column),
        ],
        out_specs=[
            pl.BlockSpec((rows, block), column),
            pl.BlockSpec((rows, block), column),
            pl.BlockSpec((8, rows), lambda j: (0, 0)),
        ],
        out_shape=[
            jax.ShapeDtypeStruct((rows, cols), BF16),
            jax.ShapeDtypeStruct((rows, cols), F32),
            jax.ShapeDtypeStruct((8, rows), F32),
        ],
        scratch_shapes=[pltpu.VMEM((rows, width), BF16), pltpu.VMEM((2, rows, HEAD_DIM), F32)],
        compiler_params=pltpu.CompilerParams(vmem_limit_bytes=24 << 20),
        name="project",
    )(got, out_weight, residual, mod_rows)


def norm_kernel(width, stream_ref, mine_ref, other_ref, mod_ref, out_ref):
    stats = mine_ref[...] + other_ref[...]
    mean = stats[0:1, :] / width
    var = stats[1:2, :] / width - mean * mean
    rows = mean.shape[1]
    mean = jnp.broadcast_to(mean, (HEAD_DIM, rows)).T
    inv = jnp.broadcast_to(lax.rsqrt(var + 1e-06), (HEAD_DIM, rows)).T
    for c in range(stream_ref.shape[1] // HEAD_DIM):
        at = slice(c * HEAD_DIM, (c + 1) * HEAD_DIM)
        shift = mod_ref[1:2, at]
        scale = mod_ref[2:3, at]
        out_ref[:, at] = ((stream_ref[:, at] - mean) * inv * (1.0 + scale) + shift).astype(BF16)


def norm(stream, mine, other, mod_rows, width):
    rows, cols = stream.shape
    block = 768
    column = lambda j: (0, j)
    whole = pl.BlockSpec((8, rows), lambda j: (0, 0))
    return pl.pallas_call(
        functools.partial(norm_kernel, width),
        grid=(cols // block,),
        in_specs=[pl.BlockSpec((rows, block), column), whole, whole, pl.BlockSpec((3, block), column)],
        out_specs=pl.BlockSpec((rows, block), column),
        out_shape=jax.ShapeDtypeStruct((rows, cols), BF16),
        compiler_params=pltpu.CompilerParams(vmem_limit_bytes=12 << 20),
        name="norm",
    )(stream, mine, other, mod_rows)


def local(residual, queries, keys, values, video_ids, timestep, modulation, out_weight):
    axes = ("seq", "mp")
    mod_rows = lax.dynamic_index_in_dim(modulation, timestep[0], 0, keepdims=False)
    spare = jnp.full(((SENT - ID) * HEAD_DIM - ROWS,), 7, jnp.int32)
    id_rows = jnp.concatenate([video_ids, spare]).reshape(SENT - ID, HEAD_DIM).astype(BF16)
    mp_index = lax.axis_index("mp").astype(jnp.int32).reshape(1)
    packed, mp_index, mod_rows = lax.optimization_barrier(
        (pack(queries, keys, values, id_rows), mp_index, mod_rows)
    )
    got = lax.all_to_all(packed, axes, 0, 0)
    back = lax.all_to_all(attend(mp_index, got), axes, 0, 0)
    hidden, stream, mine = project(back, out_weight, residual, mod_rows)
    other = lax.ppermute(mine, "mp", [(0, 1), (1, 0)])
    return hidden, norm(stream, mine, other, mod_rows, queries.shape[1])


def solution(mesh):
    return jax.shard_map(
        local,
        mesh=mesh,
        in_specs=(
            P(("dp", "seq"), "mp"),
            P(("dp", "seq", "mp"), None),
            P(("dp", "seq", "mp"), None),
            P(("dp", "seq", "mp"), None),
            P(("dp", "seq", "mp")),
            P("dp"),
            P(None, None, "mp"),
            P(None, "mp"),
        ),
        out_specs=(P(("dp", "seq"), "mp"), P(("dp", "seq"), "mp")),
        check_vma=False,
    )
```

```python
import functools
import math

import jax
import jax.numpy as jnp
from jax import lax
from jax.experimental import pallas as pl
from jax.experimental.pallas import tpu as pltpu
from jax.sharding import PartitionSpec as P

HEAD_DIM = 128
SHARDS = 16
ROWS = 192
HALF = ROWS // 2
TOKENS = SHARDS * ROWS
QF, KF, KM, VF, VM, QM, ID = 0, 192, 384, 576, 768, 960, 1056
SENT = 1072
BLOCK = 512
BACK = 3 * ROWS
TILE = 512
SPARE = -(-TILE // ROWS)
BIG = 32768.0
SCALE = math.log2(math.e) / math.sqrt(HEAD_DIM)
F32 = jnp.float32
BF16 = jnp.bfloat16


def pieces(s, m):
    full, mid = 3 * s + 2 * m, 3 * s + 1
    return (
        (0, QF, ROWS, 0, full),
        (1, KF, ROWS, 0, full),
        (1, KM, ROWS, 0, mid),
        (2, VF, ROWS, 0, full),
        (2, VM, ROWS, 0, mid),
        (0, QM, HALF, m * HALF, mid),
    )


def pack_kernel(q_ref, k_ref, v_ref, id_ref, out_ref, sem):
    given = (q_ref, k_ref, v_ref)
    for s in range(SHARDS // 2):
        for m in range(2):
            for which, to, count, row, head in pieces(s, m):
                source = given[which].at[pl.ds(row, count), pl.ds(head * HEAD_DIM, HEAD_DIM)]
                pltpu.make_async_copy(source, out_ref.at[2 * s + m, pl.ds(to, count)], sem).start()
            pltpu.make_async_copy(id_ref, out_ref.at[2 * s + m, pl.ds(ID, SENT - ID)], sem).start()
    pltpu.make_async_copy(out_ref, out_ref, sem).wait()


def pack(queries, keys, values, id_rows):
    return pl.pallas_call(
        pack_kernel,
        in_specs=[pl.BlockSpec(memory_space=pltpu.HBM)] * 3 + [pl.BlockSpec(memory_space=pl.ANY)],
        out_specs=pl.BlockSpec(memory_space=pltpu.VMEM),
        out_shape=pltpu.VMEM((SHARDS, SENT, HEAD_DIM), BF16),
        scratch_shapes=[pltpu.SemaphoreType.DMA],
        compiler_params=pltpu.CompilerParams(vmem_limit_bytes=1 << 20),
        name="pack",
    )(*(pltpu.with_memory_space_constraint(x, pltpu.HBM) for x in (queries, keys, values)), id_rows)


def attend_kernel(mp_ref, got, out_ref, qf, qm, kf, km, vf, vm, ids, is_q, is_m, is_k, score, peak, top, acc, bounds, spans, sem):
    copies = []
    for n, (first, count, ref) in enumerate(
        (
            (ID, SENT - ID, ids),
            (QF, ROWS, qf),
            (QM, HALF, qm),
            (KF, ROWS, kf),
            (KM, ROWS, km),
            (VF, ROWS, vf),
            (VM, ROWS, vm),
        )
    ):
        copy = pltpu.make_async_copy(got.at[:, pl.ds(first, count)], ref.at[pl.ds(0, SHARDS)], sem.at[n])
        copy.start()
        copies.append(copy)
    for ref in (kf, km, vf, vm):
        ref[SHARDS:] = jnp.zeros((SPARE, ROWS, HEAD_DIM), BF16)
    acc[...] = jnp.zeros_like(acc)
    top[...] = jnp.zeros_like(top)
    copies[0].wait()
    every = ids[...].astype(F32)
    for v in range(3):
        bounds[v] = jnp.sum((every <= v + 0.5).astype(F32)).astype(jnp.int32)
    c0, c1, c2 = bounds[0], bounds[1], bounds[2]
    lane = lax.broadcasted_iota(jnp.int32, (1, HEAD_DIM), 1)
    low_of = jnp.where(lane == 1, c0, jnp.where(lane == 2, c1, jnp.where(lane == 3, c2, 0)))
    end = TOKENS + SPARE * ROWS
    high_of = jnp.where(lane == 0, c0, jnp.where(lane == 1, c1, jnp.where(lane == 2, c2, jnp.where(lane == 3, TOKENS, end))))

    def inside(first, count):
        token = lax.broadcasted_iota(jnp.int32, (count, HEAD_DIM), 0) + first
        return (token >= low_of) & (token < high_of)

    def fill(b, _):
        here = inside(b * ROWS, ROWS)
        is_k[b] = jnp.where(here, 0.0, -BIG).astype(BF16)
        is_q[b] = jnp.where(here, 1.0, 0.0).astype(BF16)
        is_m[b] = jnp.where(inside(b * ROWS + mp_ref[0] * HALF, HALF), 1.0, 0.0).astype(BF16)
        return 0

    lax.fori_loop(0, SHARDS, fill, 0)
    for b in range(SHARDS, SHARDS + SPARE):
        is_k[b] = jnp.where(inside(b * ROWS, ROWS), 0.0, -BIG).astype(BF16)
    for copy in copies[1:]:
        copy.wait()

    for t in range(SHARDS // 2):
        first = t * (2 * ROWS)
        last = first + (2 * ROWS - 1)
        low = jnp.where(first >= c2, c2, jnp.where(first >= c1, c1, jnp.where(first >= c0, c0, 0)))
        high = jnp.where(last < c0, c0, jnp.where(last < c1, c1, jnp.where(last < c2, c2, TOKENS)))
        low = (low // 16) * 16
        spans[0, t] = low
        spans[1, t] = (high - low + TILE - 1) // TILE
    spans[0, SHARDS // 2] = TOKENS
    spans[1, SHARDS // 2] = 1

    def flat(ref):
        return ref.reshape(ref.shape[0] * ref.shape[1], HEAD_DIM)

    def tile_of(t):
        return jnp.minimum(t, SHARDS // 2 - 1)

    parts = ((slice(0, 2 * ROWS), qf, is_q, kf, vf), (slice(2 * ROWS, BACK), qm, is_m, km, vm))

    def look(t, key, slot):
        at = pl.ds(pl.multiple_of(key, 16), TILE)
        same = flat(is_k)[at, :]
        for rows, q_ref, is_ref, k_ref, _ in parts:
            count = rows.stop - rows.start
            mine = pl.ds(pl.multiple_of(tile_of(t) * count, count), count)
            q = jnp.concatenate([flat(q_ref)[mine, :], flat(is_ref)[mine, :]], axis=1)
            k = jnp.concatenate([flat(k_ref)[at, :], same], axis=1)
            found = lax.dot_general(q, k, (((1,), (1,)), ((), ())), preferred_element_type=F32)
            score[slot, rows] = found
            peak[slot, rows] = jnp.broadcast_to(jnp.max(found, axis=1, keepdims=True), (count, HEAD_DIM))

    def after(t, i):
        done = i + 1 == spans[1, t]
        t = jnp.where(done, jnp.minimum(t + 1, SHARDS // 2), t)
        i = jnp.where(done, 0, i + 1)
        return t, i, spans[0, t] + i * TILE

    def step(carry, slot):
        (t, i, key), (next_t, next_i, next_key) = carry
        look(next_t, next_key, 1 - slot)
        at = pl.ds(pl.multiple_of(key, 16), TILE)
        start = (i == 0) & (t < SHARDS // 2)
        ones = jnp.ones((TILE, HEAD_DIM), BF16)
        for rows, _, _, _, v_ref in parts:
            old = jnp.where(start, -1e30, top[rows])
            new = jnp.maximum(old, peak[slot, rows])
            top[rows] = new
            kept = jnp.exp2((old - new) * SCALE)
            weight = jnp.concatenate(
                [
                    jnp.exp2((score[slot, rows, c : c + HEAD_DIM] - new) * SCALE).astype(BF16)
                    for c in range(0, TILE, HEAD_DIM)
                ],
                axis=1,
            )
            v = jnp.concatenate([flat(v_ref)[at, :], ones], axis=1)
            more = jnp.dot(weight, v, preferred_element_type=F32)
            summed = acc[rows] * jnp.concatenate([kept, kept], axis=1) + more
            acc[rows] = summed
            result = (summed[:, :HEAD_DIM] / summed[:, HEAD_DIM:]).astype(BF16)
            out_ref[2 * tile_of(t), rows] = result
            out_ref[2 * tile_of(t) + 1, rows] = result
        return (next_t, next_i, next_key), after(next_t, next_i)

    total = sum(spans[1, t] for t in range(SHARDS // 2))
    begin = (0, 0, spans[0, 0])
    look(0, spans[0, 0], 0)
    lax.fori_loop(0, (total + 1) // 2, lambda _, carry: step(step(carry, 0), 1), (begin, after(0, 0)))


def attend(mp_index, got):
    rows = lambda n, spare: pltpu.VMEM((SHARDS + spare, n, HEAD_DIM), BF16)
    return pl.pallas_call(
        attend_kernel,
        in_specs=[pl.BlockSpec(memory_space=pltpu.SMEM), pl.BlockSpec(memory_space=pl.ANY)],
        out_shape=jax.ShapeDtypeStruct((SHARDS, BACK, HEAD_DIM), BF16),
        scratch_shapes=[
            rows(ROWS, 0),
            rows(HALF, 0),
            rows(ROWS, SPARE),
            rows(ROWS, SPARE),
            rows(ROWS, SPARE),
            rows(ROWS, SPARE),
            rows(SENT - ID, 0),
            rows(ROWS, 0),
            rows(HALF, 0),
            rows(ROWS, SPARE),
            pltpu.VMEM((2, BACK, TILE), F32),
            pltpu.VMEM((2, BACK, HEAD_DIM), F32),
            pltpu.VMEM((BACK, HEAD_DIM), F32),
            pltpu.VMEM((BACK, 2 * HEAD_DIM), F32),
            pltpu.SMEM((4,), jnp.int32),
            pltpu.SMEM((2, SHARDS // 2 + 1), jnp.int32),
            pltpu.SemaphoreType.DMA((7,)),
        ],
        compiler_params=pltpu.CompilerParams(vmem_limit_bytes=20 << 20),
        name="attend",
    )(mp_index, got)


def project_kernel(got, w_ref, res_ref, mod_ref, hidden_hbm, stream_ref, stat_ref, attended, hidden, sums, sem):
    for s in range(SHARDS // 2):
        mid = slice((3 * s + 1) * HEAD_DIM, (3 * s + 2) * HEAD_DIM)
        for m in range(2):
            full = slice((3 * s + 2 * m) * HEAD_DIM, (3 * s + 2 * m + 1) * HEAD_DIM)
            d = 2 * s + m
            attended[:, full] = got[d, : 2 * ROWS]
            for b in range(2):
                attended[b * ROWS + m * HALF : b * ROWS + (m + 1) * HALF, mid] = got[
                    d, 2 * ROWS + b * HALF : 2 * ROWS + (b + 1) * HALF
                ]
    sums[...] = jnp.zeros_like(sums)

    def body(j, _):
        block = pl.ds(pl.multiple_of(j * BLOCK, BLOCK), BLOCK)
        projected = jnp.dot(attended[...], w_ref[:, block], preferred_element_type=F32)
        stream = res_ref[:, block].astype(F32) + mod_ref[0:1, block] * projected
        hidden[:, block] = stream.astype(BF16)
        stream_ref[:, block] = stream
        pltpu.make_async_copy(hidden.at[:, block], hidden_hbm.at[:, block], sem.at[j]).start()
        one, two = sums[0], sums[1]
        for c in range(0, BLOCK, HEAD_DIM):
            part = stream[:, c : c + HEAD_DIM]
            one = one + part
            two = two + part * part
        sums[0] = one
        sums[1] = two
        return 0

    blocks = w_ref.shape[1] // BLOCK
    lax.fori_loop(0, blocks, body, 0)
    stat_ref[...] = jnp.zeros_like(stat_ref)
    stat_ref[0:1, :] = jnp.sum(sums[0].T, axis=0, keepdims=True)
    stat_ref[1:2, :] = jnp.sum(sums[1].T, axis=0, keepdims=True)
    for j in range(blocks):
        at = pl.ds(j * BLOCK, BLOCK)
        pltpu.make_async_copy(hidden.at[:, at], hidden_hbm.at[:, at], sem.at[j]).wait()


def project(got, out_weight, residual, mod_rows):
    width, cols = out_weight.shape
    rows = residual.shape[0]
    whole = pl.BlockSpec(memory_space=pltpu.VMEM)
    return pl.pallas_call(
        project_kernel,
        in_specs=[whole] * 4,
        out_specs=[pl.BlockSpec(memory_space=pl.ANY), whole, whole],
        out_shape=[
            jax.ShapeDtypeStruct((rows, cols), BF16),
            jax.ShapeDtypeStruct((rows, cols), F32),
            jax.ShapeDtypeStruct((8, rows), F32),
        ],
        scratch_shapes=[
            pltpu.VMEM((rows, width), BF16),
            pltpu.VMEM((rows, cols), BF16),
            pltpu.VMEM((2, rows, HEAD_DIM), F32),
            pltpu.SemaphoreType.DMA((cols // BLOCK,)),
        ],
        compiler_params=pltpu.CompilerParams(vmem_limit_bytes=24 << 20),
        name="project",
    )(got, out_weight, residual, mod_rows)


def norm_kernel(width, stream_ref, mine_ref, other_ref, mod_ref, out_ref):
    stats = mine_ref[...] + other_ref[...]
    mean = stats[0:1, :] / width
    var = stats[1:2, :] / width - mean * mean
    rows = mean.shape[1]
    mean = jnp.broadcast_to(mean, (HEAD_DIM, rows)).T
    inv = jnp.broadcast_to(lax.rsqrt(var + 1e-06), (HEAD_DIM, rows)).T
    for c in range(stream_ref.shape[1] // HEAD_DIM):
        at = slice(c * HEAD_DIM, (c + 1) * HEAD_DIM)
        shift = mod_ref[1:2, at]
        scale = mod_ref[2:3, at]
        out_ref[:, at] = ((stream_ref[:, at] - mean) * inv * (1.0 + scale) + shift).astype(BF16)


def norm(stream, mine, other, mod_rows, width):
    rows, cols = stream.shape
    block = 768
    column = lambda j: (0, j)
    whole = pl.BlockSpec((8, rows), lambda j: (0, 0))
    return pl.pallas_call(
        functools.partial(norm_kernel, width),
        grid=(cols // block,),
        in_specs=[pl.BlockSpec((rows, block), column), whole, whole, pl.BlockSpec((3, block), column)],
        out_specs=pl.BlockSpec((rows, block), column),
        out_shape=jax.ShapeDtypeStruct((rows, cols), BF16),
        compiler_params=pltpu.CompilerParams(vmem_limit_bytes=12 << 20),
        name="norm",
    )(stream, mine, other, mod_rows)


def local(residual, queries, keys, values, video_ids, timestep, modulation, out_weight):
    axes = ("seq", "mp")
    mod_rows = lax.dynamic_index_in_dim(modulation, timestep[0], 0, keepdims=False)
    spare = jnp.full(((SENT - ID) * HEAD_DIM - ROWS,), 7, jnp.int32)
    id_rows = jnp.concatenate([video_ids, spare]).reshape(SENT - ID, HEAD_DIM).astype(BF16)
    mp_index = lax.axis_index("mp").astype(jnp.int32).reshape(1)
    packed, mp_index, mod_rows = lax.optimization_barrier(
        (pack(queries, keys, values, id_rows), mp_index, mod_rows)
    )
    got = lax.all_to_all(packed, axes, 0, 0)
    back = lax.all_to_all(attend(mp_index, got), axes, 0, 0)
    hidden, stream, mine = project(back, out_weight, residual, mod_rows)
    other = lax.ppermute(mine, "mp", [(0, 1), (1, 0)])
    return hidden, norm(stream, mine, other, mod_rows, queries.shape[1])


def solution(mesh):
    return jax.shard_map(
        local,
        mesh=mesh,
        in_specs=(
            P(("dp", "seq"), "mp"),
            P(("dp", "seq", "mp"), None),
            P(("dp", "seq", "mp"), None),
            P(("dp", "seq", "mp"), None),
            P(("dp", "seq", "mp")),
            P("dp"),
            P(None, None, "mp"),
            P(None, "mp"),
        ),
        out_specs=(P(("dp", "seq"), "mp"), P(("dp", "seq"), "mp")),
        check_vma=False,
    )
```

```python
import functools
import math

import jax
import jax.numpy as jnp
from jax import lax
from jax.experimental import pallas as pl
from jax.experimental.pallas import tpu as pltpu
from jax.sharding import PartitionSpec as P

HEAD_DIM = 128
SHARDS = 16
ROWS = 192
HALF = ROWS // 2
TOKENS = SHARDS * ROWS
QF, KF, KM, VF, VM, QM, ID = 0, 192, 384, 576, 768, 960, 1056
SENT = 1064
BLOCK = 512
PART = 384
LATER = 8
BACK = 3 * ROWS
TILE = 512
SPARE = -(-TILE // ROWS)
BIG = 32768.0
SCALE = math.log2(math.e) / math.sqrt(HEAD_DIM)
F32 = jnp.float32
BF16 = jnp.bfloat16


def pieces(s, m):
    full, mid = 3 * s + 2 * m, 3 * s + 1
    return (
        (0, QF, ROWS, 0, full),
        (1, KF, ROWS, 0, full),
        (1, KM, ROWS, 0, mid),
        (2, VF, ROWS, 0, full),
        (2, VM, ROWS, 0, mid),
        (0, QM, HALF, m * HALF, mid),
    )


def pack_kernel(q_ref, k_ref, v_ref, id_ref, out_ref, sem):
    given = (q_ref, k_ref, v_ref)
    ids = id_ref[...].astype(F32).astype(BF16)
    for s in range(SHARDS // 2):
        for m in range(2):
            for which, to, count, row, head in pieces(s, m):
                source = given[which].at[pl.ds(row, count), pl.ds(head * HEAD_DIM, HEAD_DIM)]
                pltpu.make_async_copy(source, out_ref.at[2 * s + m, pl.ds(to, count)], sem).start()
            out_ref[2 * s + m, ID:] = ids
    pltpu.make_async_copy(out_ref.at[:, pl.ds(0, ID)], out_ref.at[:, pl.ds(0, ID)], sem).wait()


def pack(queries, keys, values, id_rows):
    return pl.pallas_call(
        pack_kernel,
        in_specs=[pl.BlockSpec(memory_space=pltpu.HBM)] * 3 + [pl.BlockSpec(memory_space=pltpu.VMEM)],
        out_specs=pl.BlockSpec(memory_space=pltpu.VMEM),
        out_shape=pltpu.VMEM((SHARDS, SENT, HEAD_DIM), BF16),
        scratch_shapes=[pltpu.SemaphoreType.DMA],
        compiler_params=pltpu.CompilerParams(vmem_limit_bytes=1 << 20),
        name="pack",
    )(*(pltpu.with_memory_space_constraint(x, pltpu.HBM) for x in (queries, keys, values)), id_rows)


def attend_kernel(mp_ref, got, out_ref, qf, qm, kf, km, vf, vm, ids, is_q, is_m, is_k, score, peak, top, acc, bounds, spans, sem):
    copies = []
    for n, (first, count, ref) in enumerate(
        (
            (ID, SENT - ID, ids),
            (QF, ROWS, qf),
            (QM, HALF, qm),
            (KF, ROWS, kf),
            (KM, ROWS, km),
            (VF, ROWS, vf),
            (VM, ROWS, vm),
        )
    ):
        copy = pltpu.make_async_copy(got.at[:, pl.ds(first, count)], ref.at[pl.ds(0, SHARDS)], sem.at[n])
        copy.start()
        copies.append(copy)
    for ref in (kf, km, vf, vm):
        ref[SHARDS:] = jnp.zeros((SPARE, ROWS, HEAD_DIM), BF16)
    acc[...] = jnp.zeros_like(acc)
    top[...] = jnp.zeros_like(top)
    copies[0].wait()
    every = ids[...].astype(F32)
    for v in range(3):
        bounds[v] = jnp.sum((every <= v + 0.5).astype(F32)).astype(jnp.int32)
    c0, c1, c2 = bounds[0], bounds[1], bounds[2]
    lane = lax.broadcasted_iota(jnp.int32, (1, HEAD_DIM), 1)
    low_of = jnp.where(lane == 1, c0, jnp.where(lane == 2, c1, jnp.where(lane == 3, c2, 0)))
    end = TOKENS + SPARE * ROWS
    high_of = jnp.where(lane == 0, c0, jnp.where(lane == 1, c1, jnp.where(lane == 2, c2, jnp.where(lane == 3, TOKENS, end))))

    def inside(first, count):
        row = lax.broadcasted_iota(jnp.int32, (count, HEAD_DIM), 0).astype(F32).astype(BF16)
        low, high = (jnp.clip(x - first, -1, 255).astype(F32).astype(BF16) for x in (low_of, high_of))
        return (row >= low) & (row < high)

    def fill(b, _):
        here = inside(b * ROWS, ROWS)
        is_k[b] = jnp.where(here, BF16(0.0), BF16(-BIG))
        is_q[b] = jnp.where(here, BF16(1.0), BF16(0.0))
        is_m[b] = jnp.where(inside(b * ROWS + mp_ref[0] * HALF, HALF), BF16(1.0), BF16(0.0))
        return 0

    lax.fori_loop(0, SHARDS, fill, 0, unroll=4)
    for b in range(SHARDS, SHARDS + SPARE):
        is_k[b] = jnp.where(inside(b * ROWS, ROWS), BF16(0.0), BF16(-BIG))
    for copy in copies[1:]:
        copy.wait()

    for t in range(SHARDS // 2):
        first = t * (2 * ROWS)
        last = first + (2 * ROWS - 1)
        low = jnp.where(first >= c2, c2, jnp.where(first >= c1, c1, jnp.where(first >= c0, c0, 0)))
        high = jnp.where(last < c0, c0, jnp.where(last < c1, c1, jnp.where(last < c2, c2, TOKENS)))
        low = (low // 16) * 16
        spans[0, t] = low
        spans[1, t] = (high - low + TILE - 1) // TILE
    spans[0, SHARDS // 2] = TOKENS
    spans[1, SHARDS // 2] = 1

    def flat(ref):
        return ref.reshape(ref.shape[0] * ref.shape[1], HEAD_DIM)

    def tile_of(t):
        return jnp.minimum(t, SHARDS // 2 - 1)

    parts = ((slice(0, 2 * ROWS), qf, is_q, kf, vf), (slice(2 * ROWS, BACK), qm, is_m, km, vm))

    def look(t, key, slot):
        at = pl.ds(pl.multiple_of(key, 16), TILE)
        same = flat(is_k)[at, :]
        for rows, q_ref, is_ref, k_ref, _ in parts:
            count = rows.stop - rows.start
            mine = pl.ds(pl.multiple_of(tile_of(t) * count, count), count)
            q = jnp.concatenate([flat(q_ref)[mine, :], flat(is_ref)[mine, :]], axis=1)
            k = jnp.concatenate([flat(k_ref)[at, :], same], axis=1)
            found = lax.dot_general(q, k, (((1,), (1,)), ((), ())), preferred_element_type=F32)
            score[slot, rows] = found
            peak[slot, rows] = jnp.broadcast_to(jnp.max(found, axis=1, keepdims=True), (count, HEAD_DIM))

    def after(t, i):
        done = i + 1 == spans[1, t]
        t = jnp.where(done, jnp.minimum(t + 1, SHARDS // 2), t)
        i = jnp.where(done, 0, i + 1)
        return t, i, spans[0, t] + i * TILE

    def step(carry, slot):
        (t, i, key), (next_t, next_i, next_key) = carry
        look(next_t, next_key, 1 - slot)
        at = pl.ds(pl.multiple_of(key, 16), TILE)
        start = (i == 0) & (t < SHARDS // 2)
        ones = jnp.ones((TILE, HEAD_DIM), BF16)
        for rows, _, _, _, v_ref in parts:
            old = jnp.where(start, -1e30, top[rows])
            new = jnp.maximum(old, peak[slot, rows])
            top[rows] = new
            kept = jnp.exp2((old - new) * SCALE)
            weight = jnp.concatenate(
                [
                    jnp.exp2((score[slot, rows, c : c + HEAD_DIM] - new) * SCALE).astype(BF16)
                    for c in range(0, TILE, HEAD_DIM)
                ],
                axis=1,
            )
            v = jnp.concatenate([flat(v_ref)[at, :], ones], axis=1)
            more = jnp.dot(weight, v, preferred_element_type=F32)
            summed = acc[rows] * jnp.concatenate([kept, kept], axis=1) + more
            acc[rows] = summed
            result = (summed[:, :HEAD_DIM] / summed[:, HEAD_DIM:]).astype(BF16)
            out_ref[2 * tile_of(t), rows] = result
            out_ref[2 * tile_of(t) + 1, rows] = result
        return (next_t, next_i, next_key), after(next_t, next_i)

    total = sum(spans[1, t] for t in range(SHARDS // 2))
    begin = (0, 0, spans[0, 0])
    look(0, spans[0, 0], 0)
    lax.fori_loop(0, (total + 1) // 2, lambda _, carry: step(step(carry, 0), 1), (begin, after(0, 0)))


def attend(mp_index, got):
    rows = lambda n, spare: pltpu.VMEM((SHARDS + spare, n, HEAD_DIM), BF16)
    return pl.pallas_call(
        attend_kernel,
        in_specs=[pl.BlockSpec(memory_space=pltpu.SMEM), pl.BlockSpec(memory_space=pl.ANY)],
        out_shape=jax.ShapeDtypeStruct((SHARDS, BACK, HEAD_DIM), BF16),
        scratch_shapes=[
            rows(ROWS, 0),
            rows(HALF, 0),
            rows(ROWS, SPARE),
            rows(ROWS, SPARE),
            rows(ROWS, SPARE),
            rows(ROWS, SPARE),
            rows(SENT - ID, 0),
            rows(ROWS, 0),
            rows(HALF, 0),
            rows(ROWS, SPARE),
            pltpu.VMEM((2, BACK, TILE), F32),
            pltpu.VMEM((2, BACK, HEAD_DIM), F32),
            pltpu.VMEM((BACK, HEAD_DIM), F32),
            pltpu.VMEM((BACK, 2 * HEAD_DIM), F32),
            pltpu.SMEM((4,), jnp.int32),
            pltpu.SMEM((2, SHARDS // 2 + 1), jnp.int32),
            pltpu.SemaphoreType.DMA((7,)),
        ],
        compiler_params=pltpu.CompilerParams(vmem_limit_bytes=20 << 20),
        name="attend",
    )(mp_index, got)


def pick(step, table):
    row = lax.broadcasted_iota(jnp.int32, table.shape, 0)
    return jnp.sum(jnp.where(row == step, table, 0.0), axis=0, keepdims=True)


def project_kernel(small_ref, got, w_ref, res_ref, mod_ref, hidden_hbm, stream_ref, stat_ref, rows_ref, attended, hidden, gates, sums, sem):
    blocks = w_ref.shape[1] // BLOCK
    now = small_ref[SENT - ID - 1 :, HEAD_DIM - 1 :] - LATER
    for s in range(SHARDS // 2):
        mid = slice((3 * s + 1) * HEAD_DIM, (3 * s + 2) * HEAD_DIM)
        for m in range(2):
            full = slice((3 * s + 2 * m) * HEAD_DIM, (3 * s + 2 * m + 1) * HEAD_DIM)
            d = 2 * s + m
            attended[:, full] = got[d, : 2 * ROWS]
            for b in range(2):
                attended[b * ROWS + m * HALF : b * ROWS + (m + 1) * HALF, mid] = got[
                    d, 2 * ROWS + b * HALF : 2 * ROWS + (b + 1) * HALF
                ]
    sums[...] = jnp.zeros_like(sums)
    gates[...] = pick(now, mod_ref[0])
    rows_ref[0:1, :] = pick(now, mod_ref[1])
    rows_ref[1:2, :] = 1.0 + pick(now, mod_ref[2])

    def body(j, _):
        block = pl.ds(pl.multiple_of(j * BLOCK, BLOCK), BLOCK)
        projected = jnp.dot(attended[...], w_ref[:, block], preferred_element_type=F32)
        stream = res_ref[:, block].astype(F32) + gates[:, block] * projected
        hidden[:, block] = stream.astype(BF16)
        stream_ref[:, block] = stream
        pltpu.make_async_copy(hidden.at[:, block], hidden_hbm.at[:, block], sem.at[j]).start()
        one, two = sums[0], sums[1]
        for c in range(0, BLOCK, HEAD_DIM):
            part = stream[:, c : c + HEAD_DIM]
            one = one + part
            two = two + part * part
        sums[0] = one
        sums[1] = two
        return 0

    lax.fori_loop(0, blocks, body, 0)
    stat_ref[...] = jnp.zeros_like(stat_ref)
    stat_ref[0:1, :] = jnp.sum(sums[0].T, axis=0, keepdims=True)
    stat_ref[1:2, :] = jnp.sum(sums[1].T, axis=0, keepdims=True)
    for j in range(blocks):
        at = pl.ds(j * BLOCK, BLOCK)
        pltpu.make_async_copy(hidden.at[:, at], hidden_hbm.at[:, at], sem.at[j]).wait()


def project(small, got, out_weight, residual, tables):
    width, cols = out_weight.shape
    rows = residual.shape[0]
    whole = pl.BlockSpec(memory_space=pltpu.VMEM)
    return pl.pallas_call(
        project_kernel,
        in_specs=[whole] * 5,
        out_specs=[pl.BlockSpec(memory_space=pl.ANY), whole, whole, whole],
        out_shape=[
            jax.ShapeDtypeStruct((rows, cols), BF16),
            jax.ShapeDtypeStruct((rows, cols), F32),
            jax.ShapeDtypeStruct((8, rows), F32),
            jax.ShapeDtypeStruct((8, cols), F32),
        ],
        scratch_shapes=[
            pltpu.VMEM((rows, width), BF16),
            pltpu.VMEM((rows, cols), BF16),
            pltpu.VMEM((1, cols), F32),
            pltpu.VMEM((2, rows, HEAD_DIM), F32),
            pltpu.SemaphoreType.DMA((cols // BLOCK,)),
        ],
        compiler_params=pltpu.CompilerParams(vmem_limit_bytes=24 << 20),
        name="project",
    )(small, got, out_weight, residual, tables)


def norm_kernel(width, stream_ref, mine_ref, other_ref, rows_ref, out_hbm, out, moments, sem):
    stats = mine_ref[...] + other_ref[...]
    mean = stats[0:1, :] / width
    var = stats[1:2, :] / width - mean * mean
    rows = mean.shape[1]
    moments[0] = jnp.broadcast_to(mean, (HEAD_DIM, rows)).T
    moments[1] = jnp.broadcast_to(lax.rsqrt(var + 1e-06), (HEAD_DIM, rows)).T
    parts = out.shape[1] // PART

    def body(j, _):
        for c in range(0, PART, HEAD_DIM):
            at = pl.ds(pl.multiple_of(j * PART + c, HEAD_DIM), HEAD_DIM)
            scaled = (stream_ref[:, at] - moments[0]) * moments[1] * rows_ref[1:2, at]
            out[:, at] = (scaled + rows_ref[0:1, at]).astype(BF16)
        part = pl.ds(pl.multiple_of(j * PART, PART), PART)
        pltpu.make_async_copy(out.at[:, part], out_hbm.at[:, part], sem.at[j]).start()
        return 0

    lax.fori_loop(0, parts, body, 0)
    for j in range(parts):
        part = pl.ds(j * PART, PART)
        pltpu.make_async_copy(out.at[:, part], out_hbm.at[:, part], sem.at[j]).wait()


def norm(stream, mine, other, mod_rows, width):
    return pl.pallas_call(
        functools.partial(norm_kernel, width),
        in_specs=[pl.BlockSpec(memory_space=pltpu.VMEM)] * 4,
        out_specs=pl.BlockSpec(memory_space=pl.ANY),
        out_shape=jax.ShapeDtypeStruct(stream.shape, BF16),
        scratch_shapes=[
            pltpu.VMEM(stream.shape, BF16),
            pltpu.VMEM((2, stream.shape[0], HEAD_DIM), F32),
            pltpu.SemaphoreType.DMA((stream.shape[1] // PART,)),
        ],
        compiler_params=pltpu.CompilerParams(vmem_limit_bytes=12 << 20),
        name="norm",
    )(stream, mine, other, mod_rows)


def local(residual, queries, keys, values, video_ids, timestep, modulation, out_weight):
    axes = ("seq", "mp")
    spare = jnp.full(((SENT - ID) * HEAD_DIM - ROWS - 1,), LATER, jnp.int32)
    small = jnp.concatenate([video_ids, spare, timestep + LATER]).reshape(SENT - ID, HEAD_DIM)
    mp_index = lax.axis_index("mp").astype(jnp.int32).reshape(1)
    packed, mp_index = lax.optimization_barrier((pack(queries, keys, values, small), mp_index))
    got = lax.all_to_all(packed, axes, 0, 0)
    back = lax.all_to_all(attend(mp_index, got), axes, 0, 0)
    tables = modulation.transpose(1, 0, 2)
    hidden, stream, mine, mod_rows = project(small, back, out_weight, residual, tables)
    other = lax.ppermute(mine, "mp", [(0, 1), (1, 0)])
    return hidden, norm(stream, mine, other, mod_rows, queries.shape[1])


def solution(mesh):
    return jax.shard_map(
        local,
        mesh=mesh,
        in_specs=(
            P(("dp", "seq"), "mp"),
            P(("dp", "seq", "mp"), None),
            P(("dp", "seq", "mp"), None),
            P(("dp", "seq", "mp"), None),
            P(("dp", "seq", "mp")),
            P("dp"),
            P(None, None, "mp"),
            P(None, "mp"),
        ),
        out_specs=(P(("dp", "seq"), "mp"), P(("dp", "seq"), "mp")),
        check_vma=False,
    )
```

```python
import functools
import math

import jax
import jax.numpy as jnp
from jax import lax
from jax.experimental import pallas as pl
from jax.experimental.pallas import tpu as pltpu
from jax.sharding import PartitionSpec as P

HEAD_DIM = 128
SHARDS = 16
ROWS = 192
HALF = ROWS // 2
TOKENS = SHARDS * ROWS
QF, KF, KM, VF, VM, QM, ID = 0, 192, 384, 576, 768, 960, 1056
SENT = 1064
BLOCK = 512
PART = 384
LATER = 8
BACK = 3 * ROWS
TILE = 512
SPARE = -(-TILE // ROWS)
BIG = 32768.0
SCALE = math.log2(math.e) / math.sqrt(HEAD_DIM)
F32 = jnp.float32
BF16 = jnp.bfloat16


def pieces(s, m):
    full, mid = 3 * s + 2 * m, 3 * s + 1
    return (
        (0, QF, ROWS, 0, full),
        (1, KF, ROWS, 0, full),
        (1, KM, ROWS, 0, mid),
        (2, VF, ROWS, 0, full),
        (2, VM, ROWS, 0, mid),
        (0, QM, HALF, m * HALF, mid),
    )


def pack_kernel(q_ref, k_ref, v_ref, id_ref, out_ref, sem):
    given = (q_ref, k_ref, v_ref)
    ids = id_ref[...].astype(F32).astype(BF16)
    for s in range(SHARDS // 2):
        for m in range(2):
            for which, to, count, row, head in pieces(s, m):
                source = given[which].at[pl.ds(row, count), pl.ds(head * HEAD_DIM, HEAD_DIM)]
                pltpu.make_async_copy(source, out_ref.at[2 * s + m, pl.ds(to, count)], sem).start()
            out_ref[2 * s + m, ID:] = ids
    pltpu.make_async_copy(out_ref.at[:, pl.ds(0, ID)], out_ref.at[:, pl.ds(0, ID)], sem).wait()


def pack(queries, keys, values, id_rows):
    return pl.pallas_call(
        pack_kernel,
        in_specs=[pl.BlockSpec(memory_space=pltpu.HBM)] * 3 + [pl.BlockSpec(memory_space=pltpu.VMEM)],
        out_specs=pl.BlockSpec(memory_space=pltpu.VMEM),
        out_shape=pltpu.VMEM((SHARDS, SENT, HEAD_DIM), BF16),
        scratch_shapes=[pltpu.SemaphoreType.DMA],
        compiler_params=pltpu.CompilerParams(vmem_limit_bytes=1 << 20),
        name="pack",
    )(*(pltpu.with_memory_space_constraint(x, pltpu.HBM) for x in (queries, keys, values)), id_rows)


def attend_kernel(mp_ref, got, out_ref, qf, qm, kf, km, vf, vm, ids, is_q, is_m, is_k, score, peak, top, acc, bounds, spans, sem):
    copies = []
    for n, (first, count, ref) in enumerate(
        (
            (ID, SENT - ID, ids),
            (QF, ROWS, qf),
            (QM, HALF, qm),
            (KF, ROWS, kf),
            (KM, ROWS, km),
            (VF, ROWS, vf),
            (VM, ROWS, vm),
        )
    ):
        copy = pltpu.make_async_copy(got.at[:, pl.ds(first, count)], ref.at[pl.ds(0, SHARDS)], sem.at[n])
        copy.start()
        copies.append(copy)
    for ref in (kf, km, vf, vm):
        ref[SHARDS:] = jnp.zeros((SPARE, ROWS, HEAD_DIM), BF16)
    acc[...] = jnp.zeros_like(acc)
    top[...] = jnp.zeros_like(top)
    copies[0].wait()
    every = ids[...].astype(F32)
    for v in range(3):
        bounds[v] = jnp.sum((every <= v + 0.5).astype(F32)).astype(jnp.int32)
    c0, c1, c2 = bounds[0], bounds[1], bounds[2]
    lane = lax.broadcasted_iota(jnp.int32, (1, HEAD_DIM), 1)
    low_of = jnp.where(lane == 1, c0, jnp.where(lane == 2, c1, jnp.where(lane == 3, c2, 0)))
    end = TOKENS + SPARE * ROWS
    high_of = jnp.where(lane == 0, c0, jnp.where(lane == 1, c1, jnp.where(lane == 2, c2, jnp.where(lane == 3, TOKENS, end))))

    def inside(first, count):
        row = lax.broadcasted_iota(jnp.int32, (count, HEAD_DIM), 0).astype(F32).astype(BF16)
        low, high = (jnp.clip(x - first, -1, 255).astype(F32).astype(BF16) for x in (low_of, high_of))
        return (row >= low) & (row < high)

    def fill(b, _):
        here = inside(b * ROWS, ROWS)
        is_k[b] = jnp.where(here, BF16(0.0), BF16(-BIG))
        is_q[b] = jnp.where(here, BF16(1.0), BF16(0.0))
        is_m[b] = jnp.where(inside(b * ROWS + mp_ref[0] * HALF, HALF), BF16(1.0), BF16(0.0))
        return 0

    lax.fori_loop(0, SHARDS, fill, 0, unroll=4)
    for b in range(SHARDS, SHARDS + SPARE):
        is_k[b] = jnp.where(inside(b * ROWS, ROWS), BF16(0.0), BF16(-BIG))
    for copy in copies[1:5]:
        copy.wait()

    for t in range(SHARDS // 2):
        first = t * (2 * ROWS)
        last = first + (2 * ROWS - 1)
        low = jnp.where(first >= c2, c2, jnp.where(first >= c1, c1, jnp.where(first >= c0, c0, 0)))
        high = jnp.where(last < c0, c0, jnp.where(last < c1, c1, jnp.where(last < c2, c2, TOKENS)))
        low = (low // 16) * 16
        spans[0, t] = low
        spans[1, t] = (high - low + TILE - 1) // TILE
    spans[0, SHARDS // 2] = TOKENS
    spans[1, SHARDS // 2] = 1

    def flat(ref):
        return ref.reshape(ref.shape[0] * ref.shape[1], HEAD_DIM)

    def tile_of(t):
        return jnp.minimum(t, SHARDS // 2 - 1)

    parts = ((slice(0, 2 * ROWS), qf, is_q, kf, vf), (slice(2 * ROWS, BACK), qm, is_m, km, vm))

    def look(t, key, slot):
        at = pl.ds(pl.multiple_of(key, 16), TILE)
        same = flat(is_k)[at, :]
        for rows, q_ref, is_ref, k_ref, _ in parts:
            count = rows.stop - rows.start
            mine = pl.ds(pl.multiple_of(tile_of(t) * count, count), count)
            q = jnp.concatenate([flat(q_ref)[mine, :], flat(is_ref)[mine, :]], axis=1)
            k = jnp.concatenate([flat(k_ref)[at, :], same], axis=1)
            found = lax.dot_general(q, k, (((1,), (1,)), ((), ())), preferred_element_type=F32)
            score[slot, rows] = found
            peak[slot, rows] = jnp.broadcast_to(jnp.max(found, axis=1, keepdims=True), (count, HEAD_DIM))

    def after(t, i):
        done = i + 1 == spans[1, t]
        t = jnp.where(done, jnp.minimum(t + 1, SHARDS // 2), t)
        i = jnp.where(done, 0, i + 1)
        return t, i, spans[0, t] + i * TILE

    def step(carry, slot):
        (t, i, key), (next_t, next_i, next_key) = carry
        look(next_t, next_key, 1 - slot)
        at = pl.ds(pl.multiple_of(key, 16), TILE)
        start = (i == 0) & (t < SHARDS // 2)
        ones = jnp.ones((TILE, HEAD_DIM), BF16)
        for rows, _, _, _, v_ref in parts:
            old = jnp.where(start, -1e30, top[rows])
            new = jnp.maximum(old, peak[slot, rows])
            top[rows] = new
            kept = jnp.exp2((old - new) * SCALE)
            weight = jnp.concatenate(
                [
                    jnp.exp2((score[slot, rows, c : c + HEAD_DIM] - new) * SCALE).astype(BF16)
                    for c in range(0, TILE, HEAD_DIM)
                ],
                axis=1,
            )
            v = jnp.concatenate([flat(v_ref)[at, :], ones], axis=1)
            more = jnp.dot(weight, v, preferred_element_type=F32)
            summed = acc[rows] * jnp.concatenate([kept, kept], axis=1) + more
            acc[rows] = summed
            result = (summed[:, :HEAD_DIM] / summed[:, HEAD_DIM:]).astype(BF16)
            out_ref[2 * tile_of(t), rows] = result
            out_ref[2 * tile_of(t) + 1, rows] = result
        return (next_t, next_i, next_key), after(next_t, next_i)

    total = sum(spans[1, t] for t in range(SHARDS // 2))
    begin = (0, 0, spans[0, 0])
    look(0, spans[0, 0], 0)
    for copy in copies[5:]:
        copy.wait()
    lax.fori_loop(0, (total + 1) // 2, lambda _, carry: step(step(carry, 0), 1), (begin, after(0, 0)))


def attend(mp_index, got):
    rows = lambda n, spare: pltpu.VMEM((SHARDS + spare, n, HEAD_DIM), BF16)
    return pl.pallas_call(
        attend_kernel,
        in_specs=[pl.BlockSpec(memory_space=pltpu.SMEM), pl.BlockSpec(memory_space=pl.ANY)],
        out_shape=jax.ShapeDtypeStruct((SHARDS, BACK, HEAD_DIM), BF16),
        scratch_shapes=[
            rows(ROWS, 0),
            rows(HALF, 0),
            rows(ROWS, SPARE),
            rows(ROWS, SPARE),
            rows(ROWS, SPARE),
            rows(ROWS, SPARE),
            rows(SENT - ID, 0),
            rows(ROWS, 0),
            rows(HALF, 0),
            rows(ROWS, SPARE),
            pltpu.VMEM((2, BACK, TILE), F32),
            pltpu.VMEM((2, BACK, HEAD_DIM), F32),
            pltpu.VMEM((BACK, HEAD_DIM), F32),
            pltpu.VMEM((BACK, 2 * HEAD_DIM), F32),
            pltpu.SMEM((4,), jnp.int32),
            pltpu.SMEM((2, SHARDS // 2 + 1), jnp.int32),
            pltpu.SemaphoreType.DMA((7,)),
        ],
        compiler_params=pltpu.CompilerParams(vmem_limit_bytes=20 << 20),
        name="attend",
    )(mp_index, got)


def pick(step, table):
    row = lax.broadcasted_iota(jnp.int32, table.shape, 0)
    return jnp.sum(jnp.where(row == step, table, 0.0), axis=0, keepdims=True)


def heads(got, s):
    pieces = [got[2 * s + m, (2 + b) * ROWS - b * HALF : (2 + b) * ROWS - b * HALF + HALF] for b in range(2) for m in range(2)]
    return jnp.concatenate([got[2 * s, : 2 * ROWS], jnp.concatenate(pieces, axis=0), got[2 * s + 1, : 2 * ROWS]], axis=1)


def project_kernel(small_ref, got, w_ref, res_ref, mod_ref, hidden_hbm, stream_ref, stat_ref, rows_ref, hidden, gates, sums, sem):
    blocks = w_ref.shape[1] // BLOCK
    now = small_ref[SENT - ID - 1 :, HEAD_DIM - 1 :] - LATER
    sums[...] = jnp.zeros_like(sums)
    gates[...] = pick(now, mod_ref[0])
    rows_ref[0:1, :] = pick(now, mod_ref[1])
    rows_ref[1:2, :] = 1.0 + pick(now, mod_ref[2])

    def body(j, _):
        block = pl.ds(pl.multiple_of(j * BLOCK, BLOCK), BLOCK)
        attended = jnp.concatenate([heads(got, s) for s in range(SHARDS // 2)], axis=1)
        projected = jnp.dot(attended, w_ref[:, block], preferred_element_type=F32)
        stream = res_ref[:, block].astype(F32) + gates[:, block] * projected
        hidden[:, block] = stream.astype(BF16)
        stream_ref[:, block] = stream
        pltpu.make_async_copy(hidden.at[:, block], hidden_hbm.at[:, block], sem.at[j]).start()
        one, two = sums[0], sums[1]
        for c in range(0, BLOCK, HEAD_DIM):
            part = stream[:, c : c + HEAD_DIM]
            one = one + part
            two = two + part * part
        sums[0] = one
        sums[1] = two
        return 0

    lax.fori_loop(0, blocks, body, 0)
    stat_ref[...] = jnp.zeros_like(stat_ref)
    stat_ref[0:1, :] = jnp.sum(sums[0].T, axis=0, keepdims=True)
    stat_ref[1:2, :] = jnp.sum(sums[1].T, axis=0, keepdims=True)
    for j in range(blocks):
        at = pl.ds(j * BLOCK, BLOCK)
        pltpu.make_async_copy(hidden.at[:, at], hidden_hbm.at[:, at], sem.at[j]).wait()


def project(small, got, out_weight, residual, tables):
    cols = out_weight.shape[1]
    rows = residual.shape[0]
    whole = pl.BlockSpec(memory_space=pltpu.VMEM)
    return pl.pallas_call(
        project_kernel,
        in_specs=[whole] * 5,
        out_specs=[pl.BlockSpec(memory_space=pl.ANY), whole, whole, whole],
        out_shape=[
            jax.ShapeDtypeStruct((rows, cols), BF16),
            jax.ShapeDtypeStruct((rows, cols), F32),
            jax.ShapeDtypeStruct((8, rows), F32),
            jax.ShapeDtypeStruct((8, cols), F32),
        ],
        scratch_shapes=[
            pltpu.VMEM((rows, cols), BF16),
            pltpu.VMEM((1, cols), F32),
            pltpu.VMEM((2, rows, HEAD_DIM), F32),
            pltpu.SemaphoreType.DMA((cols // BLOCK,)),
        ],
        compiler_params=pltpu.CompilerParams(vmem_limit_bytes=24 << 20),
        name="project",
    )(small, got, out_weight, residual, tables)


def norm_kernel(width, stream_ref, mine_ref, other_ref, rows_ref, out_hbm, out, moments, sem):
    stats = mine_ref[...] + other_ref[...]
    mean = stats[0:1, :] / width
    var = stats[1:2, :] / width - mean * mean
    rows = mean.shape[1]
    moments[0] = jnp.broadcast_to(mean, (HEAD_DIM, rows)).T
    moments[1] = jnp.broadcast_to(lax.rsqrt(var + 1e-06), (HEAD_DIM, rows)).T
    parts = out.shape[1] // PART

    def body(j, _):
        for c in range(0, PART, HEAD_DIM):
            at = pl.ds(pl.multiple_of(j * PART + c, HEAD_DIM), HEAD_DIM)
            scaled = (stream_ref[:, at] - moments[0]) * moments[1] * rows_ref[1:2, at]
            out[:, at] = (scaled + rows_ref[0:1, at]).astype(BF16)
        part = pl.ds(pl.multiple_of(j * PART, PART), PART)
        pltpu.make_async_copy(out.at[:, part], out_hbm.at[:, part], sem.at[j]).start()
        return 0

    lax.fori_loop(0, parts, body, 0)
    for j in range(parts):
        part = pl.ds(j * PART, PART)
        pltpu.make_async_copy(out.at[:, part], out_hbm.at[:, part], sem.at[j]).wait()


def norm(stream, mine, other, mod_rows, width):
    return pl.pallas_call(
        functools.partial(norm_kernel, width),
        in_specs=[pl.BlockSpec(memory_space=pltpu.VMEM)] * 4,
        out_specs=pl.BlockSpec(memory_space=pl.ANY),
        out_shape=jax.ShapeDtypeStruct(stream.shape, BF16),
        scratch_shapes=[
            pltpu.VMEM(stream.shape, BF16),
            pltpu.VMEM((2, stream.shape[0], HEAD_DIM), F32),
            pltpu.SemaphoreType.DMA((stream.shape[1] // PART,)),
        ],
        compiler_params=pltpu.CompilerParams(vmem_limit_bytes=12 << 20),
        name="norm",
    )(stream, mine, other, mod_rows)


def local(residual, queries, keys, values, video_ids, timestep, modulation, out_weight):
    axes = ("seq", "mp")
    spare = jnp.full(((SENT - ID) * HEAD_DIM - ROWS - 1,), LATER, jnp.int32)
    small = jnp.concatenate([video_ids, spare, timestep + LATER]).reshape(SENT - ID, HEAD_DIM)
    mp_index = lax.axis_index("mp").astype(jnp.int32).reshape(1)
    packed, mp_index = lax.optimization_barrier((pack(queries, keys, values, small), mp_index))
    got = lax.all_to_all(packed, axes, 0, 0)
    back = lax.all_to_all(attend(mp_index, got), axes, 0, 0)
    tables = modulation.transpose(1, 0, 2)
    hidden, stream, mine, mod_rows = project(small, back, out_weight, residual, tables)
    other = lax.ppermute(mine, "mp", [(0, 1), (1, 0)])
    return hidden, norm(stream, mine, other, mod_rows, queries.shape[1])


def solution(mesh):
    return jax.shard_map(
        local,
        mesh=mesh,
        in_specs=(
            P(("dp", "seq"), "mp"),
            P(("dp", "seq", "mp"), None),
            P(("dp", "seq", "mp"), None),
            P(("dp", "seq", "mp"), None),
            P(("dp", "seq", "mp")),
            P("dp"),
            P(None, None, "mp"),
            P(None, "mp"),
        ),
        out_specs=(P(("dp", "seq"), "mp"), P(("dp", "seq"), "mp")),
        check_vma=False,
    )
```

```python
import functools
import math

import jax
import jax.numpy as jnp
from jax import lax
from jax.experimental import pallas as pl
from jax.experimental.pallas import tpu as pltpu
from jax.sharding import PartitionSpec as P

HEAD_DIM = 128
SHARDS = 16
ROWS = 192
HALF = ROWS // 2
TOKENS = SHARDS * ROWS
QF, KF, KM, VF, VM, QM, ID = 0, 192, 384, 576, 768, 960, 1056
SENT = 1064
BLOCK = 512
PART = 384
LATER = 8
BACK = 3 * ROWS
TILE = 512
SPARE = -(-TILE // ROWS)
BIG = 32768.0
SCALE = math.log2(math.e) / math.sqrt(HEAD_DIM)
F32 = jnp.float32
BF16 = jnp.bfloat16


def pieces(s, m):
    full, mid = 3 * s + 2 * m, 3 * s + 1
    return (
        (0, QF, ROWS, 0, full),
        (1, KF, ROWS, 0, full),
        (1, KM, ROWS, 0, mid),
        (2, VF, ROWS, 0, full),
        (2, VM, ROWS, 0, mid),
        (0, QM, HALF, m * HALF, mid),
    )


def pack_kernel(q_ref, k_ref, v_ref, id_ref, out_ref, sem):
    given = (q_ref, k_ref, v_ref)
    ids = id_ref[...].astype(F32).astype(BF16)
    for s in range(SHARDS // 2):
        for m in range(2):
            for which, to, count, row, head in pieces(s, m):
                source = given[which].at[pl.ds(row, count), pl.ds(head * HEAD_DIM, HEAD_DIM)]
                pltpu.make_async_copy(source, out_ref.at[2 * s + m, pl.ds(to, count)], sem).start()
            out_ref[2 * s + m, ID:] = ids
    pltpu.make_async_copy(out_ref.at[:, pl.ds(0, ID)], out_ref.at[:, pl.ds(0, ID)], sem).wait()


def pack(queries, keys, values, id_rows):
    return pl.pallas_call(
        pack_kernel,
        in_specs=[pl.BlockSpec(memory_space=pltpu.HBM)] * 3 + [pl.BlockSpec(memory_space=pltpu.VMEM)],
        out_specs=pl.BlockSpec(memory_space=pltpu.VMEM),
        out_shape=pltpu.VMEM((SHARDS, SENT, HEAD_DIM), BF16),
        scratch_shapes=[pltpu.SemaphoreType.DMA],
        compiler_params=pltpu.CompilerParams(vmem_limit_bytes=1 << 20),
        name="pack",
    )(*(pltpu.with_memory_space_constraint(x, pltpu.HBM) for x in (queries, keys, values)), id_rows)


def attend_kernel(mp_ref, got, out_ref, qf, qm, kf, km, vf, vm, ids, is_q, is_m, is_k, score, peak, top, acc, bounds, spans, sem):
    copies = []
    for n, (first, count, ref) in enumerate(
        (
            (ID, SENT - ID, ids),
            (QF, ROWS, qf),
            (QM, HALF, qm),
            (KF, ROWS, kf),
            (KM, ROWS, km),
            (VF, ROWS, vf),
            (VM, ROWS, vm),
        )
    ):
        copy = pltpu.make_async_copy(got.at[:, pl.ds(first, count)], ref.at[pl.ds(0, SHARDS)], sem.at[n])
        copy.start()
        copies.append(copy)
    for ref in (kf, km, vf, vm):
        ref[SHARDS:] = jnp.zeros((SPARE, ROWS, HEAD_DIM), BF16)
    acc[...] = jnp.zeros_like(acc)
    top[...] = jnp.zeros_like(top)
    copies[0].wait()
    every = ids[...].astype(F32)
    for v in range(3):
        bounds[v] = jnp.sum((every <= v + 0.5).astype(F32)).astype(jnp.int32)
    c0, c1, c2 = bounds[0], bounds[1], bounds[2]
    lane = lax.broadcasted_iota(jnp.int32, (1, HEAD_DIM), 1)
    low_of = jnp.where(lane == 1, c0, jnp.where(lane == 2, c1, jnp.where(lane == 3, c2, 0)))
    end = TOKENS + SPARE * ROWS
    high_of = jnp.where(lane == 0, c0, jnp.where(lane == 1, c1, jnp.where(lane == 2, c2, jnp.where(lane == 3, TOKENS, end))))

    def inside(first, count):
        row = lax.broadcasted_iota(jnp.int32, (count, HEAD_DIM), 0).astype(F32).astype(BF16)
        low, high = (jnp.clip(x - first, -1, 255).astype(F32).astype(BF16) for x in (low_of, high_of))
        return (row >= low) & (row < high)

    def fill(b, _):
        here = inside(b * ROWS, ROWS)
        is_k[b] = jnp.where(here, BF16(0.0), BF16(-BIG))
        is_q[b] = jnp.where(here, BF16(1.0), BF16(0.0))
        is_m[b] = jnp.where(inside(b * ROWS + mp_ref[0] * HALF, HALF), BF16(1.0), BF16(0.0))
        return 0

    lax.fori_loop(0, SHARDS, fill, 0, unroll=4)
    for b in range(SHARDS, SHARDS + SPARE):
        is_k[b] = jnp.where(inside(b * ROWS, ROWS), BF16(0.0), BF16(-BIG))
    for copy in copies[1:5]:
        copy.wait()

    for t in range(SHARDS // 2):
        first = t * (2 * ROWS)
        last = first + (2 * ROWS - 1)
        low = jnp.where(first >= c2, c2, jnp.where(first >= c1, c1, jnp.where(first >= c0, c0, 0)))
        high = jnp.where(last < c0, c0, jnp.where(last < c1, c1, jnp.where(last < c2, c2, TOKENS)))
        low = (low // 16) * 16
        spans[0, t] = low
        spans[1, t] = (high - low + TILE - 1) // TILE
    spans[0, SHARDS // 2] = TOKENS
    spans[1, SHARDS // 2] = 1

    def flat(ref):
        return ref.reshape(ref.shape[0] * ref.shape[1], HEAD_DIM)

    def tile_of(t):
        return jnp.minimum(t, SHARDS // 2 - 1)

    parts = ((slice(0, 2 * ROWS), qf, is_q, kf, vf), (slice(2 * ROWS, BACK), qm, is_m, km, vm))

    def look(t, key, slot):
        at = pl.ds(pl.multiple_of(key, 16), TILE)
        same = flat(is_k)[at, :]
        for rows, q_ref, is_ref, k_ref, _ in parts:
            count = rows.stop - rows.start
            mine = pl.ds(pl.multiple_of(tile_of(t) * count, count), count)
            q = jnp.concatenate([flat(q_ref)[mine, :], flat(is_ref)[mine, :]], axis=1)
            k = jnp.concatenate([flat(k_ref)[at, :], same], axis=1)
            found = lax.dot_general(q, k, (((1,), (1,)), ((), ())), preferred_element_type=F32)
            score[slot, rows] = found
            peak[slot, rows] = jnp.broadcast_to(jnp.max(found, axis=1, keepdims=True), (count, HEAD_DIM))

    def after(t, i):
        done = i + 1 == spans[1, t]
        t = jnp.where(done, jnp.minimum(t + 1, SHARDS // 2), t)
        i = jnp.where(done, 0, i + 1)
        return t, i, spans[0, t] + i * TILE

    def step(carry, slot):
        (t, i, key), (next_t, next_i, next_key) = carry
        look(next_t, next_key, 1 - slot)
        at = pl.ds(pl.multiple_of(key, 16), TILE)
        start = (i == 0) & (t < SHARDS // 2)
        ones = jnp.ones((TILE, HEAD_DIM), BF16)
        for rows, _, _, _, v_ref in parts:
            old = jnp.where(start, -1e30, top[rows])
            new = jnp.maximum(old, peak[slot, rows])
            top[rows] = new
            kept = jnp.exp2((old - new) * SCALE)
            weight = jnp.concatenate(
                [
                    jnp.exp2((score[slot, rows, c : c + HEAD_DIM] - new) * SCALE).astype(BF16)
                    for c in range(0, TILE, HEAD_DIM)
                ],
                axis=1,
            )
            v = jnp.concatenate([flat(v_ref)[at, :], ones], axis=1)
            more = jnp.dot(weight, v, preferred_element_type=F32)
            summed = acc[rows] * jnp.concatenate([kept, kept], axis=1) + more
            acc[rows] = summed
            result = (summed[:, :HEAD_DIM] / summed[:, HEAD_DIM:]).astype(BF16)
            out_ref[2 * tile_of(t), rows] = result
            out_ref[2 * tile_of(t) + 1, rows] = result
        return (next_t, next_i, next_key), after(next_t, next_i)

    total = sum(spans[1, t] for t in range(SHARDS // 2))
    begin = (0, 0, spans[0, 0])
    look(0, spans[0, 0], 0)
    for copy in copies[5:]:
        copy.wait()
    lax.fori_loop(0, (total + 1) // 2, lambda _, carry: step(step(carry, 0), 1), (begin, after(0, 0)))


def attend(mp_index, got):
    rows = lambda n, spare: pltpu.VMEM((SHARDS + spare, n, HEAD_DIM), BF16)
    return pl.pallas_call(
        attend_kernel,
        in_specs=[pl.BlockSpec(memory_space=pltpu.SMEM), pl.BlockSpec(memory_space=pl.ANY)],
        out_shape=jax.ShapeDtypeStruct((SHARDS, BACK, HEAD_DIM), BF16),
        scratch_shapes=[
            rows(ROWS, 0),
            rows(HALF, 0),
            rows(ROWS, SPARE),
            rows(ROWS, SPARE),
            rows(ROWS, SPARE),
            rows(ROWS, SPARE),
            rows(SENT - ID, 0),
            rows(ROWS, 0),
            rows(HALF, 0),
            rows(ROWS, SPARE),
            pltpu.VMEM((2, BACK, TILE), F32),
            pltpu.VMEM((2, BACK, HEAD_DIM), F32),
            pltpu.VMEM((BACK, HEAD_DIM), F32),
            pltpu.VMEM((BACK, 2 * HEAD_DIM), F32),
            pltpu.SMEM((4,), jnp.int32),
            pltpu.SMEM((2, SHARDS // 2 + 1), jnp.int32),
            pltpu.SemaphoreType.DMA((7,)),
        ],
        compiler_params=pltpu.CompilerParams(vmem_limit_bytes=20 << 20),
        name="attend",
    )(mp_index, got)


def pick(small_ref, table):
    step = small_ref[SENT - ID - 1 :, HEAD_DIM - 1 :] - LATER
    row = lax.broadcasted_iota(jnp.int32, table.shape, 0)
    return jnp.sum(jnp.where(row == step, table, 0.0), axis=0, keepdims=True)


def heads(got, s):
    pieces = [got[2 * s + m, (2 + b) * ROWS - b * HALF : (2 + b) * ROWS - b * HALF + HALF] for b in range(2) for m in range(2)]
    return jnp.concatenate([got[2 * s, : 2 * ROWS], jnp.concatenate(pieces, axis=0), got[2 * s + 1, : 2 * ROWS]], axis=1)


def project_kernel(small_ref, got, w_ref, res_ref, mod_ref, stream_ref, stat_ref, gates, sums):
    sums[...] = jnp.zeros_like(sums)
    gates[...] = pick(small_ref, mod_ref[0])

    def body(j, _):
        block = pl.ds(pl.multiple_of(j * BLOCK, BLOCK), BLOCK)
        attended = jnp.concatenate([heads(got, s) for s in range(SHARDS // 2)], axis=1)
        projected = jnp.dot(attended, w_ref[:, block], preferred_element_type=F32)
        stream = res_ref[:, block].astype(F32) + gates[:, block] * projected
        stream_ref[:, block] = stream
        one, two = sums[0], sums[1]
        for c in range(0, BLOCK, HEAD_DIM):
            part = stream[:, c : c + HEAD_DIM]
            one = one + part
            two = two + part * part
        sums[0] = one
        sums[1] = two
        return 0

    lax.fori_loop(0, w_ref.shape[1] // BLOCK, body, 0)
    stat_ref[...] = jnp.zeros_like(stat_ref)
    stat_ref[0:1, :] = jnp.sum(sums[0].T, axis=0, keepdims=True)
    stat_ref[1:2, :] = jnp.sum(sums[1].T, axis=0, keepdims=True)


def project(small, got, out_weight, residual, tables):
    cols = out_weight.shape[1]
    rows = residual.shape[0]
    whole = pl.BlockSpec(memory_space=pltpu.VMEM)
    return pl.pallas_call(
        project_kernel,
        in_specs=[whole] * 5,
        out_specs=[whole, whole],
        out_shape=[jax.ShapeDtypeStruct((rows, cols), F32), jax.ShapeDtypeStruct((8, rows), F32)],
        scratch_shapes=[pltpu.VMEM((1, cols), F32), pltpu.VMEM((2, rows, HEAD_DIM), F32)],
        compiler_params=pltpu.CompilerParams(vmem_limit_bytes=24 << 20),
        name="project",
    )(small, got, out_weight, residual, tables)


def emit_kernel(small_ref, stream_ref, mod_ref, hidden_hbm, rows_ref, hidden, sem):
    parts = hidden.shape[1] // PART

    def body(j, _):
        part = pl.ds(pl.multiple_of(j * PART, PART), PART)
        hidden[:, part] = stream_ref[:, part].astype(BF16)
        pltpu.make_async_copy(hidden.at[:, part], hidden_hbm.at[:, part], sem.at[j]).start()
        return 0

    lax.fori_loop(0, parts, body, 0)
    rows_ref[0:1, :] = pick(small_ref, mod_ref[1])
    rows_ref[1:2, :] = 1.0 + pick(small_ref, mod_ref[2])
    for j in range(parts):
        part = pl.ds(j * PART, PART)
        pltpu.make_async_copy(hidden.at[:, part], hidden_hbm.at[:, part], sem.at[j]).wait()


def emit(small, stream, tables):
    whole = pl.BlockSpec(memory_space=pltpu.VMEM)
    return pl.pallas_call(
        emit_kernel,
        in_specs=[whole] * 3,
        out_specs=[pl.BlockSpec(memory_space=pl.ANY), whole],
        out_shape=[
            jax.ShapeDtypeStruct(stream.shape, BF16),
            jax.ShapeDtypeStruct((8, stream.shape[1]), F32),
        ],
        scratch_shapes=[pltpu.VMEM(stream.shape, BF16), pltpu.SemaphoreType.DMA((stream.shape[1] // PART,))],
        compiler_params=pltpu.CompilerParams(vmem_limit_bytes=8 << 20),
        name="emit",
    )(small, stream, tables)


def norm_kernel(width, stream_ref, mine_ref, other_ref, rows_ref, out_hbm, out, moments, sem):
    stats = mine_ref[...] + other_ref[...]
    mean = stats[0:1, :] / width
    var = stats[1:2, :] / width - mean * mean
    rows = mean.shape[1]
    moments[0] = jnp.broadcast_to(mean, (HEAD_DIM, rows)).T
    moments[1] = jnp.broadcast_to(lax.rsqrt(var + 1e-06), (HEAD_DIM, rows)).T
    parts = out.shape[1] // PART

    def body(j, _):
        for c in range(0, PART, HEAD_DIM):
            at = pl.ds(pl.multiple_of(j * PART + c, HEAD_DIM), HEAD_DIM)
            scaled = (stream_ref[:, at] - moments[0]) * moments[1] * rows_ref[1:2, at]
            out[:, at] = (scaled + rows_ref[0:1, at]).astype(BF16)
        part = pl.ds(pl.multiple_of(j * PART, PART), PART)
        pltpu.make_async_copy(out.at[:, part], out_hbm.at[:, part], sem.at[j]).start()
        return 0

    lax.fori_loop(0, parts, body, 0)
    for j in range(parts):
        part = pl.ds(j * PART, PART)
        pltpu.make_async_copy(out.at[:, part], out_hbm.at[:, part], sem.at[j]).wait()


def norm(stream, mine, other, mod_rows, width):
    return pl.pallas_call(
        functools.partial(norm_kernel, width),
        in_specs=[pl.BlockSpec(memory_space=pltpu.VMEM)] * 4,
        out_specs=pl.BlockSpec(memory_space=pl.ANY),
        out_shape=jax.ShapeDtypeStruct(stream.shape, BF16),
        scratch_shapes=[
            pltpu.VMEM(stream.shape, BF16),
            pltpu.VMEM((2, stream.shape[0], HEAD_DIM), F32),
            pltpu.SemaphoreType.DMA((stream.shape[1] // PART,)),
        ],
        compiler_params=pltpu.CompilerParams(vmem_limit_bytes=12 << 20),
        name="norm",
    )(stream, mine, other, mod_rows)


def local(residual, queries, keys, values, video_ids, timestep, modulation, out_weight):
    axes = ("seq", "mp")
    spare = jnp.full(((SENT - ID) * HEAD_DIM - ROWS - 1,), LATER, jnp.int32)
    small = jnp.concatenate([video_ids, spare, timestep + LATER]).reshape(SENT - ID, HEAD_DIM)
    mp_index = lax.axis_index("mp").astype(jnp.int32).reshape(1)
    packed, mp_index = lax.optimization_barrier((pack(queries, keys, values, small), mp_index))
    got = lax.all_to_all(packed, axes, 0, 0)
    back = lax.all_to_all(attend(mp_index, got), axes, 0, 0)
    tables = modulation.transpose(1, 0, 2)
    stream, mine = project(small, back, out_weight, residual, tables)
    other = lax.ppermute(mine, "mp", [(0, 1), (1, 0)])
    hidden, mod_rows = emit(small, stream, tables)
    return hidden, norm(stream, mine, other, mod_rows, queries.shape[1])


def solution(mesh):
    return jax.shard_map(
        local,
        mesh=mesh,
        in_specs=(
            P(("dp", "seq"), "mp"),
            P(("dp", "seq", "mp"), None),
            P(("dp", "seq", "mp"), None),
            P(("dp", "seq", "mp"), None),
            P(("dp", "seq", "mp")),
            P("dp"),
            P(None, None, "mp"),
            P(None, "mp"),
        ),
        out_specs=(P(("dp", "seq"), "mp"), P(("dp", "seq"), "mp")),
        check_vma=False,
    )
```
